32 devices in a mesh: wide: 16 (over z, y, x), narrow: 2 (over core).
Axes of the slice: x: 2, y: 2, z: 4, core: 2. Of those that a mesh axis runs over, the one named last changes fastest.
Arguments:
- positions: float32 [3, 8192], P(None, ('wide', 'narrow')), may hold values from 0 to 1
- forces: float32 [3, 16, 8192], P(None, None, ('wide', 'narrow')), may hold values from -6 to 6
- waves: int32 [3, 8192], replicated, may hold values from -16 to 16, as said below
Outputs:
- velocity: float32 [3, 16, 8192], P(None, None, ('wide', 'narrow'))
The draws below stay inside these ranges and needn't reach their ends.
Inputs may be any that keep to these rules, and one draw needn't show every extreme that they name: `waves`: no wavevector is (0, 0, 0).
All inputs are finite; a program needn't handle non-finite values.
Results may differ from the reference program's by a relative error of at most 0.0053.
Values may be sent and summed in bfloat16 or wider, within the bound.
No kernel may reach another device: no remote copies, remote signals or barrier semaphores. Data moves between devices by JAX's collectives and lax.ppermute only.
A program may use at most 64 MiB of HBM per device.

```python
import jax
import jax.numpy as jnp
from jax import lax

PROBES = 16
KWAVES = 8192
NTOT = 8192


def draw_waves(key, part):
    values = jax.random.randint(jax.random.fold_in(key, 7), (3, KWAVES), -16, 17).astype(jnp.int32)
    zero = (values[0] == 0) & (values[1] == 0) & (values[2] == 0)
    first = jnp.where(zero, 1, values[0]).astype(jnp.int32)
    values = jnp.stack([first, values[1], values[2]])
    corner = jnp.array([-16, 16, -16], jnp.int32)
    return values.at[:, 0].set(corner)


def shard_levels(stream_key, shape, shards, smallest, high):
    factor_of, own = 1.0, jax.random.fold_in(stream_key, 6)
    for dim, blocks in shards:
        heights = jnp.exp(jax.random.uniform(jax.random.fold_in(own, dim), (blocks,), jnp.float32, smallest / len(shards), high / len(shards)))
        factor_of = factor_of * jnp.repeat(heights, shape[dim] // blocks).reshape([-1 if axis == dim else 1 for axis in range(len(shape))])
    return factor_of


def scatter_about(rng, extent, deviation, bound, shards=(), kind=jnp.bfloat16):
    values = deviation * jax.random.normal(rng, extent, jnp.float32)
    if shards:
        values = values * shard_levels(rng, extent, shards, -0.22, 0.18)
    return jnp.clip(values, -bound, bound).astype(kind)


def setup_inputs(seed: int = 0) -> dict:
    keys = jax.random.split(jax.random.key(seed), 4)
    positions = jnp.clip(1.0 * jax.random.uniform(keys[0], (3, NTOT), jnp.float32) ** shard_levels(keys[0], (3, NTOT), ((1, 32),), -0.2, 0.2), 0.0, 1.0)
    forces = scatter_about(keys[1], (3, PROBES, NTOT), 1.0, 6.0, ((2, 32),), jnp.float32)
    waves = draw_waves(jax.random.fold_in(keys[3], 71), 0)
    return dict(positions=positions, forces=forces, waves=waves)


two_pi = 6.283185307179586
radius = 0.005
xi_split = 40.0

def make_tables(wblock, positions):
    mf = wblock.astype(jnp.float32)
    theta = two_pi * (mf[0][:, None] * positions[0][None, :] + mf[1][:, None] * positions[1][None, :] + mf[2][:, None] * positions[2][None, :])
    return (jnp.cos(theta).astype(jnp.bfloat16), jnp.sin(theta).astype(jnp.bfloat16))

def scale_sums(sums, wblock, amp):
    cols = sums.shape[1]
    split = sums.reshape(2, 3, -1, cols)
    kvec = two_pi * wblock.astype(jnp.float32)
    ksq = lax.optimization_barrier(jnp.sum(kvec * kvec, axis=0))
    inner = lax.optimization_barrier(jnp.sum(kvec[None, :, None, :] * split, axis=1))
    proj = split - kvec[None, :, None, :] * (inner / ksq)[:, None, :, :]
    qarg = ksq / (4.0 * xi_split * xi_split)
    factor = amp * (1.0 - radius * radius * ksq / 3.0) * (1.0 + qarg + 2.0 * qarg * qarg) * jnp.exp(-qarg) / ksq
    return (proj * factor).reshape(sums.shape[0], cols).astype(jnp.bfloat16)

def reference(positions, forces, waves):
    ntot = positions.shape[1]
    kwaves = waves.shape[1]
    force_bf = forces.reshape(-1, ntot).astype(jnp.bfloat16)
    width = 64
    blocks = waves.reshape(3, kwaves // width, width).transpose(1, 0, 2)

    def forward(wblock):
        cosine, sine = make_tables(wblock, positions)
        dims = (((1,), (1,)), ((), ()))
        sc = lax.dot_general(force_bf, cosine, dims, preferred_element_type=jnp.float32)
        ss = lax.dot_general(force_bf, sine, dims, preferred_element_type=jnp.float32)
        return jnp.concatenate([sc, ss], axis=0)
    sums = lax.map(forward, blocks)
    sums = sums.transpose(1, 0, 2).reshape(-1, kwaves)
    amp = 20000.0 / jnp.sqrt(jnp.float32(ntot) * jnp.float32(kwaves))
    scaled = scale_sums(sums, waves, amp)
    half = force_bf.shape[0]
    sblocks = scaled.reshape(2 * half, kwaves // width, width).transpose(1, 0, 2)

    def backward(total, items):
        wblock, piece = items
        cosine, sine = make_tables(wblock, positions)
        total = total + jnp.dot(piece[:half], cosine, preferred_element_type=jnp.float32)
        total = total + jnp.dot(piece[half:], sine, preferred_element_type=jnp.float32)
        return (total, None)
    total, _ = lax.scan(backward, jnp.zeros((half, ntot), jnp.float32), (blocks, sblocks))
    return total.reshape(forces.shape)
```

```python
import functools

import jax
import jax.numpy as jnp
from jax import lax
from jax.experimental import pallas as pl
from jax.experimental.pallas import tpu as pltpu
from jax.sharding import PartitionSpec as P

two_pi = 6.283185307179586
radius = 0.005
xi_split = 40.0
AXES = ("wide", "narrow")
VMEM = pltpu.VMEM
SMEM = pltpu.SMEM
f32, bf16 = jnp.float32, jnp.bfloat16

SIN = (4.442867901617319, -7.307443368323551, 3.594787581869042, -0.7843727161608242)
COS = (1.414213496635887, -6.9788509910181, 5.739461197516664, -1.8835630614207908, 0.31069820075132315)
ROUND = 12582912.0
HEAD = 16


def horner(coeffs, q):
    total = coeffs[-1] * q + coeffs[-2]
    for c in reversed(coeffs[:-2]):
        total = total * q + c
    return total


def full(shape_dtype):
    return pl.BlockSpec(memory_space=VMEM)


def call(kernel, out_shape, n_in, name, smem=0, scratch=(), flops=0):
    many = isinstance(out_shape, (list, tuple))
    return pl.pallas_call(
        kernel,
        out_shape=out_shape,
        in_specs=[pl.BlockSpec(memory_space=SMEM)] * smem + [pl.BlockSpec(memory_space=VMEM)] * n_in,
        out_specs=[pl.BlockSpec(memory_space=VMEM)] * len(out_shape) if many else pl.BlockSpec(memory_space=VMEM),
        scratch_shapes=scratch,
        name=name,
        compiler_params=pltpu.CompilerParams(vmem_limit_bytes=40 << 20),
        cost_estimate=pl.CostEstimate(flops=flops, bytes_accessed=flops // 256, transcendentals=0),
    )


def split3(x):
    hi = x.astype(bf16)
    rest = x - hi.astype(f32)
    mid = rest.astype(bf16)
    low = (rest - mid.astype(f32)).astype(bf16)
    return hi, mid, low


def pack_kernel(pos_ref, force_ref, out_ref):
    hi, mid, low = split3(pos_ref[...])
    rows = out_ref.shape[1]
    parts = [hi.astype(f32), mid.astype(f32), low.astype(f32), jnp.zeros((HEAD - 9, rows), f32)]
    out_ref[:HEAD, :] = jnp.concatenate(parts, axis=0).astype(bf16)
    for a in range(force_ref.shape[0]):
        p = force_ref.shape[1]
        out_ref[HEAD + a * p : HEAD + (a + 1) * p, :] = force_ref[a].astype(bf16)


def table_kernel(chunk, amp, idx_ref, waves_ref, *refs):
    blocks = refs[:-5]
    tab_ref, acc_ref, send_ref, frame_ref, wt_ref = refs[-5:]
    kwaves = tab_ref.shape[1]
    rows = tab_ref.shape[2]
    probes = acc_ref.shape[0] // 4
    first = pl.multiple_of(idx_ref[0] * kwaves, 128)
    m = waves_ref[:, pl.ds(first, kwaves)].astype(f32)
    msq = jnp.sum(m * m, axis=0, keepdims=True)
    n = m * lax.rsqrt(msq)
    nx, ny, nz = n[0:1], n[1:2], n[2:3]
    sign = jnp.where(nz >= 0.0, 1.0, -1.0)
    a = -1.0 / (sign + nz)
    b = nx * ny * a
    ksq = (two_pi * two_pi) * msq
    qarg = ksq / (4.0 * xi_split * xi_split)
    factor = amp * (1.0 - radius * radius * ksq / 3.0) * (1.0 + qarg + 2.0 * qarg * qarg) * jnp.exp(-qarg) / ksq
    frame_ref[...] = jnp.concatenate(
        [1.0 + sign * nx * nx * a, sign * b, -sign * nx, b, sign + ny * ny * a, -ny, factor, jnp.zeros_like(b)], axis=0
    )
    head = jnp.concatenate([m, m, m, jnp.zeros((HEAD - 9, kwaves), f32)], axis=0)
    wt_ref[...] = jnp.transpose(head).astype(bf16)
    packed = []
    for ref in blocks:
        if len(ref.shape) == 2:
            packed.append(ref[...])
        else:
            packed.extend(ref[j] for j in range(ref.shape[0]))
    width = packed[0].shape[1]
    phases = [p[:HEAD] for p in packed]
    forces = jnp.concatenate([p[HEAD:] for p in packed], axis=1)
    strip = 32

    def step(c, carry):
        base = pl.multiple_of(c * chunk, chunk)

        def inner(t, carry):
            row = pl.multiple_of(base + t * strip, strip)
            w = wt_ref[pl.ds(row, strip), :]
            for j, ph in enumerate(phases):
                u = jnp.dot(w, ph, preferred_element_type=f32)
                r = u - ((u + ROUND) - ROUND)
                q = r * r
                s = r * horner(SIN, q)
                co = horner(COS, q)
                tab_ref[0, pl.ds(row, strip), j * width : (j + 1) * width] = (1.0 - s * s).astype(bf16)
                tab_ref[1, pl.ds(row, strip), j * width : (j + 1) * width] = (s * co).astype(bf16)
            return carry

        lax.fori_loop(0, chunk // strip, inner, 0, unroll=True)
        cols = pl.ds(base, chunk)
        fr = frame_ref[:, cols]
        for part in range(2):
            t = tab_ref[part, cols, :]
            sums = lax.dot_general(forces, t, (((1,), (1,)), ((), ())), preferred_element_type=f32)
            for j in range(2):
                value = sum(fr[3 * j + x : 3 * j + x + 1] * sums[x * probes : (x + 1) * probes] for x in range(3))
                low = (2 * part + j) * probes
                acc_ref[low : low + probes, cols] = value
                send_ref[low : low + probes, cols] = value.astype(bf16)
        return carry

    lax.fori_loop(0, kwaves // chunk, step, 0)


def back_kernel(chunk, acc_ref, recv_ref, frame_ref, tab_ref, out_ref):
    kwaves = tab_ref.shape[1]
    probes = acc_ref.shape[0] // 4
    out_ref[...] = jnp.zeros_like(out_ref)

    def step(c, carry):
        cols = pl.ds(pl.multiple_of(c * chunk, chunk), chunk)
        fr = frame_ref[:, cols]
        sums = acc_ref[:, cols] + recv_ref[:, cols].astype(f32)
        total = out_ref[...]
        for part in range(2):
            t0 = fr[6:7] * sums[2 * part * probes : (2 * part + 1) * probes]
            t1 = fr[6:7] * sums[(2 * part + 1) * probes : (2 * part + 2) * probes]
            scaled = jnp.concatenate([fr[x : x + 1] * t0 + fr[3 + x : 4 + x] * t1 for x in range(3)], axis=0).astype(bf16)
            total = total + jnp.dot(scaled, tab_ref[part, cols, :], preferred_element_type=f32)
        out_ref[...] = total
        return carry

    lax.fori_loop(0, kwaves // chunk, step, 0)


def shards(positions, forces, waves):
    wide, narrow = lax.axis_size("wide"), lax.axis_size("narrow")
    devices = wide * narrow
    bits = devices.bit_length() - 1
    assert devices == 1 << bits and bits >= 2
    rows = positions.shape[1]
    kwaves = waves.shape[1]
    half = forces.shape[0] * forces.shape[1]
    probes = forces.shape[1]
    top = devices >> 1
    amp = 20000.0 / float(rows * devices * kwaves) ** 0.5

    def swap(x, bit):
        return lax.ppermute(x, AXES, [(d, d ^ bit) for d in range(devices)])

    me = lax.axis_index(AXES)
    block = 2 * (me // top) + me % 2
    mine = kwaves // 4
    own = call(pack_kernel, jax.ShapeDtypeStruct((HEAD + half, rows), bf16), 2, "pack")(positions, forces)
    far = swap(own, top)
    near = swap(jnp.stack([own, far]), 1)
    pairs = mine * 4 * rows
    chunk = 256
    tab, acc, send, frame = call(
        functools.partial(table_kernel, chunk, amp),
        (
            jax.ShapeDtypeStruct((2, mine, 4 * rows), bf16),
            jax.ShapeDtypeStruct((4 * probes, mine), f32),
            jax.ShapeDtypeStruct((4 * probes, mine), bf16),
            jax.ShapeDtypeStruct((8, mine), f32),
        ),
        4,
        "table",
        smem=1,
        scratch=[VMEM((mine, HEAD), bf16)],
        flops=pairs * 4 * half,
    )(block.reshape(1), waves, own, far, near)
    bit = 2
    while bit < top:
        got = swap(send, bit)
        bit *= 2
        if bit < top:
            acc = acc + got.astype(f32)
            send = acc.astype(bf16)
    part = call(functools.partial(back_kernel, chunk), jax.ShapeDtypeStruct((half, 4 * rows), f32), 4, "back", flops=pairs * 4 * half)(
        acc, got, frame, tab
    )
    there = swap(part[:, 2 * rows :].astype(bf16), 1)
    part = part[:, : 2 * rows] + there.astype(f32)
    there = swap(part[:, rows:].astype(bf16), top)
    total = part[:, :rows] + there.astype(f32)
    return total.reshape(forces.shape)


def solution(mesh):
    placed = (P(None, AXES), P(None, None, AXES), P())
    return jax.shard_map(
        shards,
        mesh=mesh,
        in_specs=placed,
        out_specs=P(None, None, AXES),
        check_vma=False,
    )
```

```python
import functools

import jax
import jax.numpy as jnp
from jax import lax
from jax.experimental import pallas as pl
from jax.experimental.pallas import tpu as pltpu
from jax.sharding import PartitionSpec as P

two_pi = 6.283185307179586
radius = 0.005
xi_split = 40.0
AXES = ("wide", "narrow")
VMEM = pltpu.VMEM
SMEM = pltpu.SMEM
f32, bf16 = jnp.float32, jnp.bfloat16

SIN = (4.442867901617319, -7.307443368323551, 3.594787581869042, -0.7843727161608242)
COS = (1.414213496635887, -6.9788509910181, 5.739461197516664, -1.8835630614207908, 0.31069820075132315)
ROUND = 12582912.0
HEAD = 16


def horner(coeffs, q):
    total = coeffs[-1] * q + coeffs[-2]
    for c in reversed(coeffs[:-2]):
        total = total * q + c
    return total


def full(shape_dtype):
    return pl.BlockSpec(memory_space=VMEM)


def call(kernel, out_shape, n_in, name, smem=0, scratch=(), flops=0):
    many = isinstance(out_shape, (list, tuple))
    return pl.pallas_call(
        kernel,
        out_shape=out_shape,
        in_specs=[pl.BlockSpec(memory_space=SMEM)] * smem + [pl.BlockSpec(memory_space=VMEM)] * n_in,
        out_specs=[pl.BlockSpec(memory_space=VMEM)] * len(out_shape) if many else pl.BlockSpec(memory_space=VMEM),
        scratch_shapes=scratch,
        name=name,
        compiler_params=pltpu.CompilerParams(vmem_limit_bytes=40 << 20),
        cost_estimate=pl.CostEstimate(flops=flops, bytes_accessed=flops // 256, transcendentals=0),
    )


def split3(x):
    hi = x.astype(bf16)
    rest = x - hi.astype(f32)
    mid = rest.astype(bf16)
    low = (rest - mid.astype(f32)).astype(bf16)
    return hi, mid, low


def pack_kernel(pos_ref, force_ref, out_ref):
    hi, mid, low = split3(pos_ref[...])
    rows = out_ref.shape[1]
    parts = [hi.astype(f32), mid.astype(f32), low.astype(f32), jnp.zeros((HEAD - 9, rows), f32)]
    out_ref[:HEAD, :] = jnp.concatenate(parts, axis=0).astype(bf16)
    for a in range(force_ref.shape[0]):
        p = force_ref.shape[1]
        out_ref[HEAD + a * p : HEAD + (a + 1) * p, :] = force_ref[a].astype(bf16)


def frame_kernel(amp, idx_ref, waves_ref, frame_ref, wt_ref, own_ref, sem):
    kwaves = own_ref.shape[1]
    first = pl.multiple_of(idx_ref[0] * kwaves, 128)
    copy = pltpu.make_async_copy(waves_ref.at[:, pl.ds(first, kwaves)], own_ref, sem)
    copy.start()
    copy.wait()
    m = own_ref[...].astype(f32)
    msq = jnp.sum(m * m, axis=0, keepdims=True)
    n = m * lax.rsqrt(msq)
    nx, ny, nz = n[0:1], n[1:2], n[2:3]
    sign = jnp.where(nz >= 0.0, 1.0, -1.0)
    a = -1.0 / (sign + nz)
    b = nx * ny * a
    ksq = (two_pi * two_pi) * msq
    qarg = ksq / (4.0 * xi_split * xi_split)
    factor = amp * (1.0 - radius * radius * ksq / 3.0) * (1.0 + qarg + 2.0 * qarg * qarg) * jnp.exp(-qarg) / ksq
    frame_ref[...] = jnp.concatenate(
        [1.0 + sign * nx * nx * a, sign * b, -sign * nx, b, sign + ny * ny * a, -ny, factor, jnp.zeros_like(b)], axis=0
    )
    head = jnp.concatenate([m, m, m, jnp.zeros((HEAD - 9, kwaves), f32)], axis=0)
    wt_ref[...] = jnp.transpose(head).astype(bf16)


def table_kernel(chunk, frame_ref, wt_ref, *refs):
    blocks = refs[:-3]
    tab_ref, acc_ref, send_ref = refs[-3:]
    kwaves = tab_ref.shape[1]
    probes = acc_ref.shape[0] // 4
    packed = []
    for ref in blocks:
        if len(ref.shape) == 2:
            packed.append(ref[...])
        else:
            packed.extend(ref[j] for j in range(ref.shape[0]))
    width = packed[0].shape[1]
    phases = [p[:HEAD] for p in packed]
    forces = jnp.concatenate([p[HEAD:] for p in packed], axis=1)
    strip = 32

    def step(c, carry):
        base = pl.multiple_of(c * chunk, chunk)

        def inner(t, carry):
            row = pl.multiple_of(base + t * strip, strip)
            w = wt_ref[pl.ds(row, strip), :]
            for j, ph in enumerate(phases):
                u = jnp.dot(w, ph, preferred_element_type=f32)
                r = u - ((u + ROUND) - ROUND)
                q = r * r
                s = r * horner(SIN, q)
                co = horner(COS, q)
                tab_ref[0, pl.ds(row, strip), j * width : (j + 1) * width] = (1.0 - s * s).astype(bf16)
                tab_ref[1, pl.ds(row, strip), j * width : (j + 1) * width] = (s * co).astype(bf16)
            return carry

        lax.fori_loop(0, chunk // strip, inner, 0, unroll=True)
        cols = pl.ds(base, chunk)
        fr = frame_ref[:, cols]
        for part in range(2):
            t = tab_ref[part, cols, :]
            sums = lax.dot_general(forces, t, (((1,), (1,)), ((), ())), preferred_element_type=f32)
            for j in range(2):
                value = sum(fr[3 * j + x : 3 * j + x + 1] * sums[x * probes : (x + 1) * probes] for x in range(3))
                low = (2 * part + j) * probes
                acc_ref[low : low + probes, cols] = value
                send_ref[low : low + probes, cols] = value.astype(bf16)
        return carry

    lax.fori_loop(0, kwaves // chunk, step, 0)


def back_kernel(chunk, acc_ref, recv_ref, frame_ref, tab_ref, out_ref):
    kwaves = tab_ref.shape[1]
    probes = acc_ref.shape[0] // 4
    out_ref[...] = jnp.zeros_like(out_ref)

    def step(c, carry):
        cols = pl.ds(pl.multiple_of(c * chunk, chunk), chunk)
        fr = frame_ref[:, cols]
        sums = acc_ref[:, cols] + recv_ref[:, cols].astype(f32)
        total = out_ref[...]
        for part in range(2):
            t0 = fr[6:7] * sums[2 * part * probes : (2 * part + 1) * probes]
            t1 = fr[6:7] * sums[(2 * part + 1) * probes : (2 * part + 2) * probes]
            scaled = jnp.concatenate([fr[x : x + 1] * t0 + fr[3 + x : 4 + x] * t1 for x in range(3)], axis=0).astype(bf16)
            total = total + jnp.dot(scaled, tab_ref[part, cols, :], preferred_element_type=f32)
        out_ref[...] = total
        return carry

    lax.fori_loop(0, kwaves // chunk, step, 0)


def shards(positions, forces, waves):
    wide, narrow = lax.axis_size("wide"), lax.axis_size("narrow")
    devices = wide * narrow
    bits = devices.bit_length() - 1
    assert devices == 1 << bits and bits >= 2
    rows = positions.shape[1]
    kwaves = waves.shape[1]
    half = forces.shape[0] * forces.shape[1]
    probes = forces.shape[1]
    top = devices >> 1
    amp = 20000.0 / float(rows * devices * kwaves) ** 0.5

    def swap(x, bit):
        return lax.ppermute(x, AXES, [(d, d ^ bit) for d in range(devices)])

    me = lax.axis_index(AXES)
    block = 2 * (me // top) + me % 2
    mine = kwaves // 4
    own = call(pack_kernel, jax.ShapeDtypeStruct((HEAD + half, rows), bf16), 2, "pack")(positions, forces)
    far = swap(own, top)
    near = swap(jnp.stack([own, far]), 1)
    pairs = mine * 4 * rows
    chunk = 256
    frame, wt = pl.pallas_call(
        functools.partial(frame_kernel, amp),
        out_shape=(jax.ShapeDtypeStruct((8, mine), f32), jax.ShapeDtypeStruct((mine, HEAD), bf16)),
        in_specs=[pl.BlockSpec(memory_space=SMEM), pl.BlockSpec(memory_space=pl.ANY)],
        out_specs=[pl.BlockSpec(memory_space=VMEM)] * 2,
        scratch_shapes=[VMEM((3, mine), jnp.int32), pltpu.SemaphoreType.DMA],
        name="frame",
        cost_estimate=pl.CostEstimate(flops=mine * 1000, bytes_accessed=mine * 1000, transcendentals=0),
    )(block.reshape(1), waves)
    tab, acc, send = call(
        functools.partial(table_kernel, chunk),
        (
            jax.ShapeDtypeStruct((2, mine, 4 * rows), bf16),
            jax.ShapeDtypeStruct((4 * probes, mine), f32),
            jax.ShapeDtypeStruct((4 * probes, mine), bf16),
        ),
        5,
        "table",
        flops=pairs * 4 * half,
    )(frame, wt, own, far, near)
    middle = [1 << j for j in range(1, bits - 1)]
    for j in range(len(middle)):
        turn = [middle[(j + core) % len(middle)] for core in range(2)]
        got = lax.ppermute(send, AXES, [(d, d ^ turn[d % 2]) for d in range(devices)])
        if j + 1 < len(middle):
            acc = acc + got.astype(f32)
            send = acc.astype(bf16)
    part = call(functools.partial(back_kernel, chunk), jax.ShapeDtypeStruct((half, 4 * rows), f32), 4, "back", flops=pairs * 4 * half)(
        acc, got, frame, tab
    )
    there = swap(part[:, 2 * rows :].astype(bf16), 1)
    part = part[:, : 2 * rows] + there.astype(f32)
    there = swap(part[:, rows:].astype(bf16), top)
    total = part[:, :rows] + there.astype(f32)
    return total.reshape(forces.shape)


def solution(mesh):
    placed = (P(None, AXES), P(None, None, AXES), P())
    return jax.shard_map(
        shards,
        mesh=mesh,
        in_specs=placed,
        out_specs=P(None, None, AXES),
        check_vma=False,
    )
```

```python
import functools

import jax
import jax.numpy as jnp
from jax import lax
from jax.experimental import pallas as pl
from jax.experimental.pallas import tpu as pltpu
from jax.sharding import PartitionSpec as P

two_pi = 6.283185307179586
radius = 0.005
xi_split = 40.0
AXES = ("wide", "narrow")
VMEM = pltpu.VMEM
SMEM = pltpu.SMEM
f32, bf16 = jnp.float32, jnp.bfloat16

SIN = (4.442867901617319, -7.307443368323551, 3.594787581869042, -0.7843727161608242)
COS = (1.414213496635887, -6.9788509910181, 5.739461197516664, -1.8835630614207908, 0.31069820075132315)
ROUND = 12582912.0
HEAD = 16


def horner(coeffs, q):
    total = coeffs[-1] * q + coeffs[-2]
    for c in reversed(coeffs[:-2]):
        total = total * q + c
    return total


def call(kernel, out_shape, name, specs, scratch=(), flops=0):
    many = isinstance(out_shape, (list, tuple))
    spaces = {"v": VMEM, "s": SMEM, "h": pl.ANY}
    return pl.pallas_call(
        kernel,
        out_shape=out_shape,
        in_specs=[pl.BlockSpec(memory_space=spaces[x]) for x in specs],
        out_specs=[pl.BlockSpec(memory_space=VMEM)] * len(out_shape) if many else pl.BlockSpec(memory_space=VMEM),
        scratch_shapes=scratch,
        name=name,
        compiler_params=pltpu.CompilerParams(vmem_limit_bytes=24 << 20),
        cost_estimate=pl.CostEstimate(flops=flops, bytes_accessed=flops // 256, transcendentals=0),
    )


def split3(x):
    hi = x.astype(bf16)
    rest = x - hi.astype(f32)
    mid = rest.astype(bf16)
    low = (rest - mid.astype(f32)).astype(bf16)
    return hi, mid, low


def pack_kernel(pos_ref, force_ref, out_ref):
    hi, mid, low = split3(pos_ref[...])
    rows = out_ref.shape[1]
    parts = [hi.astype(f32), mid.astype(f32), low.astype(f32), jnp.zeros((HEAD - 9, rows), f32)]
    out_ref[:HEAD, :] = jnp.concatenate(parts, axis=0).astype(bf16)
    for a in range(force_ref.shape[0]):
        p = force_ref.shape[1]
        out_ref[HEAD + a * p : HEAD + (a + 1) * p, :] = force_ref[a].astype(bf16)


def frame_kernel(amp, idx_ref, waves_ref, frame_ref, wt_ref, own_ref, sem):
    kwaves = own_ref.shape[1]
    first = pl.multiple_of(idx_ref[0] * kwaves, 128)
    copy = pltpu.make_async_copy(waves_ref.at[:, pl.ds(first, kwaves)], own_ref, sem)
    copy.start()
    copy.wait()
    m = own_ref[...].astype(f32)
    msq = jnp.sum(m * m, axis=0, keepdims=True)
    n = m * lax.rsqrt(msq)
    nx, ny, nz = n[0:1], n[1:2], n[2:3]
    sign = jnp.where(nz >= 0.0, 1.0, -1.0)
    a = -1.0 / (sign + nz)
    b = nx * ny * a
    ksq = (two_pi * two_pi) * msq
    qarg = ksq / (4.0 * xi_split * xi_split)
    factor = amp * (1.0 - radius * radius * ksq / 3.0) * (1.0 + qarg + 2.0 * qarg * qarg) * jnp.exp(-qarg) / ksq
    frame_ref[...] = jnp.concatenate(
        [1.0 + sign * nx * nx * a, sign * b, -sign * nx, b, sign + ny * ny * a, -ny, factor, jnp.zeros_like(b)], axis=0
    )
    head = jnp.concatenate([m, m, m, jnp.zeros((HEAD - 9, kwaves), f32)], axis=0)
    wt_ref[...] = jnp.transpose(head).astype(bf16)


def trig(w, phase, tab_ref, rows, cols):
    u = jnp.dot(w, phase, preferred_element_type=f32)
    r = u - ((u + ROUND) - ROUND)
    q = r * r
    s = r * horner(SIN, q)
    tab_ref[0, rows, cols] = (1.0 - s * s).astype(bf16)
    tab_ref[1, rows, cols] = (s * horner(COS, q)).astype(bf16)


def trig_kernel(first, wt_ref, pack_ref, tab_ref):
    strip = 64
    phase = pack_ref[:HEAD]

    def step(t, carry):
        row = pl.multiple_of(t * strip, strip)
        trig(wt_ref[pl.ds(first + row, strip), :], phase, tab_ref, pl.ds(row, strip), slice(None))
        return carry

    lax.fori_loop(0, tab_ref.shape[1] // strip, step, 0, unroll=4)


def unpacked(refs):
    blocks = []
    for ref in refs:
        blocks.extend([ref[...]] if len(ref.shape) == 2 else [ref[j] for j in range(ref.shape[0])])
    return blocks


def sums_kernel(first, offsets, chunk, frame_ref, wt_ref, *refs):
    count = len(offsets)
    ready, packs, todo = refs[:count], refs[count : 2 * count], refs[2 * count : -3]
    tab_ref, acc_ref, send_ref = refs[-3:]
    kwaves = tab_ref.shape[1]
    probes = acc_ref.shape[0] // 4
    blocks = unpacked(todo)
    width = blocks[0].shape[1]
    forces = jnp.concatenate([b[HEAD:] for b in blocks], axis=1)
    strip = 32

    def step(c, carry):
        base = pl.multiple_of(c * chunk, chunk)
        for t in range(chunk // strip):
            row = pl.multiple_of(base + t * strip, strip)
            w = wt_ref[pl.ds(first + row, strip), :]
            for j, block in enumerate(blocks):
                trig(w, block[:HEAD], tab_ref, pl.ds(row, strip), slice(j * width, (j + 1) * width))
        fr = frame_ref[:, pl.ds(first + base, chunk)]
        for part in range(2):
            sums = jnp.zeros((3 * probes, chunk), f32)
            for offset, table, pack in zip(offsets, ready, packs):
                t = table[part, pl.ds(offset + base, chunk), :]
                sums += lax.dot_general(pack[HEAD:], t, (((1,), (1,)), ((), ())), preferred_element_type=f32)
            t = tab_ref[part, pl.ds(base, chunk), :]
            sums += lax.dot_general(forces, t, (((1,), (1,)), ((), ())), preferred_element_type=f32)
            for j in range(2):
                value = sum(fr[3 * j + x : 3 * j + x + 1] * sums[x * probes : (x + 1) * probes] for x in range(3))
                low = (2 * part + j) * probes
                acc_ref[low : low + probes, pl.ds(base, chunk)] = value
                send_ref[low : low + probes, pl.ds(base, chunk)] = value.astype(bf16)
        return carry

    lax.fori_loop(0, kwaves // chunk, step, 0)


def back_kernel(first, offsets, chunk, last, acc_ref, recv_ref, frame_ref, *refs):
    tables = refs[: len(offsets)]
    rest = refs[len(offsets) :]
    kwaves = acc_ref.shape[1]
    probes = acc_ref.shape[0] // 4
    halves = []
    for part in range(2):
        cols = slice(first, first + kwaves)
        t0, t1 = (
            frame_ref[6:7, cols] * (acc_ref[low : low + probes] + recv_ref[low : low + probes].astype(f32))
            for low in (2 * part * probes, (2 * part + 1) * probes)
        )
        halves.append(
            jnp.concatenate([frame_ref[x : x + 1, cols] * t0 + frame_ref[3 + x : 4 + x, cols] * t1 for x in range(3)], axis=0).astype(bf16)
        )
    begin = 0
    for offset, table in zip(offsets, tables):
        width = table.shape[2]
        total = sum(
            jnp.dot(halves[part], table[part, offset : offset + kwaves, :], preferred_element_type=f32) for part in range(2)
        )
        if not last:
            rest[0][:, begin : begin + width] = total
            begin += width
            continue
        earlier, keep, send = rest
        total += earlier[:, begin : begin + width]
        split = keep.shape[1]
        if begin < split:
            keep[:, begin : min(begin + width, split)] = total[:, : split - begin]
        if begin + width > split:
            low = max(begin, split)
            send[:, low - split : begin + width - split] = total[:, low - begin :].astype(bf16)
        begin += width


def shards(positions, forces, waves):
    wide, narrow = lax.axis_size("wide"), lax.axis_size("narrow")
    devices = wide * narrow
    bits = devices.bit_length() - 1
    assert devices == 1 << bits and bits >= 2
    rows = positions.shape[1]
    kwaves = waves.shape[1]
    half = forces.shape[0] * forces.shape[1]
    probes = forces.shape[1]
    top = devices >> 1
    amp = 20000.0 / float(rows * devices * kwaves) ** 0.5

    def swap(x, bit):
        return lax.ppermute(x, AXES, [(d, d ^ bit) for d in range(devices)])

    me = lax.axis_index(AXES)
    block = 2 * (me // top) + me % 2
    mine = kwaves // 4
    part = mine // 2
    fl = 4 * half * rows
    shape = jax.ShapeDtypeStruct
    own = call(pack_kernel, shape((HEAD + half, rows), bf16), "pack", "vv")(positions, forces)
    far = swap(own, top)
    frame, wt = call(
        functools.partial(frame_kernel, amp),
        (shape((8, mine), f32), shape((mine, HEAD), bf16)),
        "frame",
        "sh",
        scratch=[VMEM((3, mine), jnp.int32), pltpu.SemaphoreType.DMA],
        flops=mine * 1000,
    )(block.reshape(1), waves)
    tab_own = call(functools.partial(trig_kernel, 0), shape((2, mine, rows), bf16), "trig_own", "vv", flops=mine * fl)(wt, own)
    both, tab_own, frame, wt = lax.optimization_barrier((jnp.stack([own, far]), tab_own, frame, wt))
    near = swap(both, 1)
    tab_far = call(functools.partial(trig_kernel, 0), shape((2, part, rows), bf16), "trig_far", "vv", flops=part * fl)(wt, far)

    def sums(first, offsets, ready, packs, todo, width):
        return call(
            functools.partial(sums_kernel, first, offsets, 256),
            (shape((2, part, width), bf16), shape((4 * probes, part), f32), shape((4 * probes, part), bf16)),
            "sums",
            "v" * (2 + 2 * len(ready) + len(todo)),
            flops=part * fl * (width // rows),
        )(frame, wt, *ready, *packs, *todo)

    middle = [1 << j for j in range(1, bits - 1)]
    steps = len(middle)

    def exchange(x, j, chunk):
        turn = [middle[(j + core + 2 * chunk) % steps] for core in range(2)]
        return lax.ppermute(x, AXES, [(d, d ^ turn[d % 2]) for d in range(devices)])

    tab_a, acc_a, send_a = sums(0, (0, 0), (tab_own, tab_far), (own, far), (near,), 2 * rows)
    tab_b, acc_b, send_b = sums(part, (part,), (tab_own,), (own,), (far, near), 3 * rows)
    state = [[acc_a, send_a, None], [acc_b, send_b, None]]
    for j in range(steps):
        for chunk in range(2):
            acc, send, _ = state[chunk]
            got = exchange(send, j, chunk)
            if j + 1 < steps:
                acc = acc + got.astype(f32)
                send = acc.astype(bf16)
            state[chunk] = [acc, send, got]
    first = call(
        functools.partial(back_kernel, 0, (0, 0, 0), 256, False), shape((half, 4 * rows), f32), "back", "vvvvvv", flops=part * fl * 4
    )(state[0][0], state[0][2], frame, tab_own, tab_far, tab_a)
    keep, send = call(
        functools.partial(back_kernel, part, (part, 0), 256, True),
        (shape((half, 2 * rows), f32), shape((half, 2 * rows), bf16)),
        "back",
        "vvvvvv",
        flops=part * fl * 4,
    )(state[1][0], state[1][2], frame, tab_own, tab_b, first)
    there = swap(send, 1)
    keep = keep + there.astype(f32)
    there = swap(keep[:, rows:].astype(bf16), top)
    total = keep[:, :rows] + there.astype(f32)
    return total.reshape(forces.shape)


def solution(mesh):
    placed = (P(None, AXES), P(None, None, AXES), P())
    return jax.shard_map(
        shards,
        mesh=mesh,
        in_specs=placed,
        out_specs=P(None, None, AXES),
        check_vma=False,
    )
```

```python
import functools

import jax
import jax.numpy as jnp
from jax import lax
from jax.experimental import pallas as pl
from jax.experimental.pallas import tpu as pltpu
from jax.sharding import PartitionSpec as P

two_pi = 6.283185307179586
radius = 0.005
xi_split = 40.0
AXES = ("wide", "narrow")
VMEM = pltpu.VMEM
SMEM = pltpu.SMEM
f32, bf16 = jnp.float32, jnp.bfloat16

SIN = (4.442867901617319, -7.307443368323551, 3.594787581869042, -0.7843727161608242)
ROUND = 12582912.0
TINY = 1e-30
HEAD = 16


def horner(coeffs, q):
    total = coeffs[-1] * q + coeffs[-2]
    for c in reversed(coeffs[:-2]):
        total = total * q + c
    return total


def call(kernel, out_shape, name, specs, scratch=(), flops=0):
    many = isinstance(out_shape, (list, tuple))
    spaces = {"v": VMEM, "s": SMEM, "h": pltpu.HBM}
    return pl.pallas_call(
        kernel,
        out_shape=out_shape,
        in_specs=[pl.BlockSpec(memory_space=spaces[x]) for x in specs],
        out_specs=[pl.BlockSpec(memory_space=VMEM)] * len(out_shape) if many else pl.BlockSpec(memory_space=VMEM),
        scratch_shapes=scratch,
        name=name,
        compiler_params=pltpu.CompilerParams(vmem_limit_bytes=24 << 20),
        cost_estimate=pl.CostEstimate(flops=flops, bytes_accessed=flops // 256, transcendentals=0),
    )


def split3(x):
    hi = x.astype(bf16)
    rest = x - hi.astype(f32)
    mid = rest.astype(bf16)
    low = (rest - mid.astype(f32)).astype(bf16)
    return hi, mid, low


def pack_kernel(idx_ref, pos_hbm, force_hbm, waves_hbm, out_ref, own_ref, pos_ref, force_ref, sems):
    first = pl.multiple_of(idx_ref[0] * own_ref.shape[1], 128)
    copies = [
        pltpu.make_async_copy(pos_hbm, pos_ref, sems.at[0]),
        pltpu.make_async_copy(force_hbm, force_ref, sems.at[1]),
        pltpu.make_async_copy(waves_hbm.at[:, pl.ds(first, own_ref.shape[1])], own_ref, sems.at[2]),
    ]
    for copy in copies:
        copy.start()
    for copy in copies:
        copy.wait()
    hi, mid, low = split3(pos_ref[...])
    rows = out_ref.shape[1]
    parts = [hi.astype(f32), mid.astype(f32), low.astype(f32), jnp.zeros((HEAD - 9, rows), f32)]
    out_ref[:HEAD, :] = jnp.concatenate(parts, axis=0).astype(bf16)
    for a in range(force_ref.shape[0]):
        p = force_ref.shape[1]
        out_ref[HEAD + a * p : HEAD + (a + 1) * p, :] = force_ref[a].astype(bf16)


def frame_kernel(amp, own_ref, frame_ref, wt_ref):
    kwaves = own_ref.shape[1]
    m = own_ref[...].astype(f32)
    msq = jnp.sum(m * m, axis=0, keepdims=True)
    n = m * lax.rsqrt(msq)
    nx, ny, nz = n[0:1], n[1:2], n[2:3]
    sign = jnp.where(nz >= 0.0, 1.0, -1.0)
    a = -1.0 / (sign + nz)
    b = nx * ny * a
    ksq = (two_pi * two_pi) * msq
    qarg = ksq / (4.0 * xi_split * xi_split)
    factor = amp * (1.0 - radius * radius * ksq / 3.0) * (1.0 + qarg + 2.0 * qarg * qarg) * jnp.exp(-qarg) / ksq
    frame_ref[...] = jnp.concatenate(
        [1.0 + sign * nx * nx * a, sign * b, -sign * nx, b, sign + ny * ny * a, -ny, factor, jnp.zeros_like(b)], axis=0
    )
    head = jnp.concatenate([m, m, m, jnp.zeros((HEAD - 9, kwaves), f32)], axis=0)
    wt_ref[...] = jnp.transpose(head).astype(bf16)


def trig(w, phase, tab_ref, rows, cols):
    u = jnp.dot(w, phase, preferred_element_type=f32)
    r = u - ((u + ROUND) - ROUND)
    s = r * horner(SIN, r * r)
    square = s * s
    tab_ref[0, rows, cols] = (1.0 - square).astype(bf16)
    rest = jnp.maximum(2.0 - square, TINY)
    tab_ref[1, rows, cols] = (s * (rest * lax.rsqrt(rest))).astype(bf16)


def trig_kernel(first, wt_ref, pack_ref, tab_ref):
    strip = 64
    phase = pack_ref[:HEAD]

    def step(t, carry):
        row = pl.multiple_of(t * strip, strip)
        trig(wt_ref[pl.ds(first + row, strip), :], phase, tab_ref, pl.ds(row, strip), slice(None))
        return carry

    lax.fori_loop(0, tab_ref.shape[1] // strip, step, 0, unroll=4)


def unpacked(refs):
    blocks = []
    for ref in refs:
        blocks.extend([ref[...]] if len(ref.shape) == 2 else [ref[j] for j in range(ref.shape[0])])
    return blocks


def sums_kernel(first, offsets, chunk, frame_ref, wt_ref, *refs):
    count = len(offsets)
    ready, packs, todo = refs[:count], refs[count : 2 * count], refs[2 * count : -3]
    tab_ref, acc_ref, send_ref = refs[-3:]
    kwaves = tab_ref.shape[1]
    probes = acc_ref.shape[0] // 4
    blocks = unpacked(todo)
    width = blocks[0].shape[1]
    forces = jnp.concatenate([b[HEAD:] for b in blocks], axis=1)
    strip = 32

    def step(c, carry):
        base = pl.multiple_of(c * chunk, chunk)
        for t in range(chunk // strip):
            row = pl.multiple_of(base + t * strip, strip)
            w = wt_ref[pl.ds(first + row, strip), :]
            for j, block in enumerate(blocks):
                trig(w, block[:HEAD], tab_ref, pl.ds(row, strip), slice(j * width, (j + 1) * width))
        fr = frame_ref[:, pl.ds(first + base, chunk)]
        for part in range(2):
            sums = jnp.zeros((3 * probes, chunk), f32)
            for offset, table, pack in zip(offsets, ready, packs):
                t = table[part, pl.ds(offset + base, chunk), :]
                sums += lax.dot_general(pack[HEAD:], t, (((1,), (1,)), ((), ())), preferred_element_type=f32)
            t = tab_ref[part, pl.ds(base, chunk), :]
            sums += lax.dot_general(forces, t, (((1,), (1,)), ((), ())), preferred_element_type=f32)
            for j in range(2):
                value = sum(fr[3 * j + x : 3 * j + x + 1] * sums[x * probes : (x + 1) * probes] for x in range(3))
                low = (2 * part + j) * probes
                acc_ref[low : low + probes, pl.ds(base, chunk)] = value
                send_ref[low : low + probes, pl.ds(base, chunk)] = value.astype(bf16)
        return carry

    lax.fori_loop(0, kwaves // chunk, step, 0)


def back_kernel(first, offsets, chunk, last, acc_ref, recv_ref, frame_ref, *refs):
    tables = refs[: len(offsets)]
    rest = refs[len(offsets) :]
    kwaves = acc_ref.shape[1]
    probes = acc_ref.shape[0] // 4
    halves = []
    for part in range(2):
        cols = slice(first, first + kwaves)
        t0, t1 = (
            frame_ref[6:7, cols] * (acc_ref[low : low + probes] + recv_ref[low : low + probes].astype(f32))
            for low in (2 * part * probes, (2 * part + 1) * probes)
        )
        halves.append(
            jnp.concatenate([frame_ref[x : x + 1, cols] * t0 + frame_ref[3 + x : 4 + x, cols] * t1 for x in range(3)], axis=0).astype(bf16)
        )
    begin = 0
    for offset, table in zip(offsets, tables):
        width = table.shape[2]
        total = sum(
            jnp.dot(halves[part], table[part, offset : offset + kwaves, :], preferred_element_type=f32) for part in range(2)
        )
        if not last:
            rest[0][:, begin : begin + width] = total
            begin += width
            continue
        earlier, keep, send = rest
        total += earlier[:, begin : begin + width]
        split = keep.shape[1]
        if begin < split:
            keep[:, begin : min(begin + width, split)] = total[:, : split - begin]
        if begin + width > split:
            low = max(begin, split)
            send[:, low - split : begin + width - split] = total[:, low - begin :].astype(bf16)
        begin += width


def shards(positions, forces, waves):
    wide, narrow = lax.axis_size("wide"), lax.axis_size("narrow")
    devices = wide * narrow
    bits = devices.bit_length() - 1
    assert devices == 1 << bits and bits >= 2
    rows = positions.shape[1]
    kwaves = waves.shape[1]
    half = forces.shape[0] * forces.shape[1]
    probes = forces.shape[1]
    top = devices >> 1
    amp = 20000.0 / float(rows * devices * kwaves) ** 0.5

    def swap(x, bit):
        return lax.ppermute(x, AXES, [(d, d ^ bit) for d in range(devices)])

    me = lax.axis_index(AXES)
    block = 2 * (me // top) + me % 2
    mine = kwaves // 4
    fl = 4 * half * rows
    shape = jax.ShapeDtypeStruct
    own, owned = call(
        pack_kernel,
        (shape((HEAD + half, rows), bf16), shape((3, mine), jnp.int32)),
        "pack",
        "shhh",
        scratch=[VMEM(positions.shape, f32), VMEM(forces.shape, f32), pltpu.SemaphoreType.DMA((3,))],
    )(block.reshape(1), *(pltpu.with_memory_space_constraint(x, pltpu.HBM) for x in (positions, forces, waves)))
    far = swap(own, top)
    frame, wt = call(
        functools.partial(frame_kernel, amp), (shape((8, mine), f32), shape((mine, HEAD), bf16)), "frame", "v", flops=mine * 1000
    )(owned)
    tab_own = call(functools.partial(trig_kernel, 0), shape((2, mine, rows), bf16), "trig_own", "vv", flops=mine * fl)(wt, own)
    both, tab_own, frame, wt = lax.optimization_barrier((jnp.stack([own, far]), tab_own, frame, wt))
    near = swap(both, 1)
    split = mine * 5 // 8 // 256 * 256
    parts = (split, mine - split)

    def trig_call(name, first, count, pack):
        return call(functools.partial(trig_kernel, first), shape((2, count, rows), bf16), name, "vv", flops=count * fl)(wt, pack)

    def sums(first, count, offsets, ready, packs, todo, width):
        return call(
            functools.partial(sums_kernel, first, offsets, 256),
            (shape((2, count, width), bf16), shape((4 * probes, count), f32), shape((4 * probes, count), bf16)),
            "sums",
            "v" * (2 + 2 * len(ready) + len(todo)),
            flops=count * fl * (width // rows),
        )(frame, wt, *ready, *packs, *todo)

    middle = [1 << j for j in range(1, bits - 1)]
    steps = len(middle)

    def exchange(x, j, chunk):
        turn = [middle[(j + core + 2 * chunk) % steps] for core in range(2)]
        return lax.ppermute(x, AXES, [(d, d ^ turn[d % 2]) for d in range(devices)])

    tab_far = trig_call("trig_far", 0, split, far)
    tab_a, acc_a, send_a = sums(0, parts[0], (0, 0), (tab_own, tab_far), (own, far), (near,), 2 * rows)
    tab_b, acc_b, send_b = sums(split, parts[1], (split,), (tab_own,), (own,), (far, near), 3 * rows)
    state = [[acc_a, send_a, None], [acc_b, send_b, None]]
    for j in range(steps):
        for chunk in range(2):
            acc, send, _ = state[chunk]
            got = exchange(send, j, chunk)
            if j + 1 < steps:
                acc = acc + got.astype(f32)
                send = acc.astype(bf16)
            state[chunk] = [acc, send, got]
    first = call(
        functools.partial(back_kernel, 0, (0, 0, 0), 256, False), shape((half, 4 * rows), f32), "back", "vvvvvv", flops=parts[0] * fl * 4
    )(state[0][0], state[0][2], frame, tab_own, tab_far, tab_a)
    keep, send = call(
        functools.partial(back_kernel, split, (split, 0), 256, True),
        (shape((half, 2 * rows), f32), shape((half, 2 * rows), bf16)),
        "back",
        "vvvvvv",
        flops=parts[1] * fl * 4,
    )(state[1][0], state[1][2], frame, tab_own, tab_b, first)
    there = swap(send, 1)
    keep = keep + there.astype(f32)
    there = swap(keep[:, rows:].astype(bf16), top)
    total = keep[:, :rows] + there.astype(f32)
    return total.reshape(forces.shape)


def solution(mesh):
    placed = (P(None, AXES), P(None, None, AXES), P())
    return jax.shard_map(
        shards,
        mesh=mesh,
        in_specs=placed,
        out_specs=P(None, None, AXES),
        check_vma=False,
    )
```

```python
import functools

import jax
import jax.numpy as jnp
from jax import lax
from jax.experimental import pallas as pl
from jax.experimental.pallas import tpu as pltpu
from jax.sharding import PartitionSpec as P

two_pi = 6.283185307179586
radius = 0.005
xi_split = 40.0
AXES = ("wide", "narrow")
VMEM = pltpu.VMEM
SMEM = pltpu.SMEM
f32, bf16 = jnp.float32, jnp.bfloat16

SIN = (4.442867901617319, -7.307443368323551, 3.594787581869042, -0.7843727161608242)
ROUND = 12582912.0
TINY = 1e-30
PACE = 2
HEAD = 16


def horner(coeffs, q):
    total = coeffs[-1] * q + coeffs[-2]
    for c in reversed(coeffs[:-2]):
        total = total * q + c
    return total


def call(kernel, out_shape, name, specs, scratch=(), flops=0):
    many = isinstance(out_shape, (list, tuple))
    spaces = {"v": VMEM, "s": SMEM, "h": pltpu.HBM}
    return pl.pallas_call(
        kernel,
        out_shape=out_shape,
        in_specs=[pl.BlockSpec(memory_space=spaces[x]) for x in specs],
        out_specs=[pl.BlockSpec(memory_space=VMEM)] * len(out_shape) if many else pl.BlockSpec(memory_space=VMEM),
        scratch_shapes=scratch,
        name=name,
        compiler_params=pltpu.CompilerParams(vmem_limit_bytes=24 << 20),
        cost_estimate=pl.CostEstimate(flops=flops, bytes_accessed=flops // 256, transcendentals=0),
    )


def split3(x):
    hi = x.astype(bf16)
    rest = x - hi.astype(f32)
    mid = rest.astype(bf16)
    low = (rest - mid.astype(f32)).astype(bf16)
    return hi, mid, low


def pack_kernel(idx_ref, pos_hbm, force_hbm, waves_hbm, out_ref, own_ref, pos_ref, force_ref, sems):
    first = pl.multiple_of(idx_ref[0] * own_ref.shape[1], 128)
    copies = [
        pltpu.make_async_copy(pos_hbm, pos_ref, sems.at[0]),
        pltpu.make_async_copy(force_hbm, force_ref, sems.at[1]),
        pltpu.make_async_copy(waves_hbm.at[:, pl.ds(first, own_ref.shape[1])], own_ref, sems.at[2]),
    ]
    for copy in copies:
        copy.start()
    for copy in copies:
        copy.wait()
    hi, mid, low = split3(pos_ref[...])
    rows = out_ref.shape[1]
    parts = [hi.astype(f32), mid.astype(f32), low.astype(f32), jnp.zeros((HEAD - 9, rows), f32)]
    out_ref[:HEAD, :] = jnp.concatenate(parts, axis=0).astype(bf16)
    for a in range(force_ref.shape[0]):
        p = force_ref.shape[1]
        out_ref[HEAD + a * p : HEAD + (a + 1) * p, :] = force_ref[a].astype(bf16)


def frame_kernel(amp, own_ref, frame_ref, wt_ref):
    kwaves = own_ref.shape[1]
    m = own_ref[...].astype(f32)
    msq = jnp.sum(m * m, axis=0, keepdims=True)
    n = m * lax.rsqrt(msq)
    nx, ny, nz = n[0:1], n[1:2], n[2:3]
    sign = jnp.where(nz >= 0.0, 1.0, -1.0)
    a = -1.0 / (sign + nz)
    b = nx * ny * a
    ksq = (two_pi * two_pi) * msq
    qarg = ksq / (4.0 * xi_split * xi_split)
    factor = amp * (1.0 - radius * radius * ksq / 3.0) * (1.0 + qarg + 2.0 * qarg * qarg) * jnp.exp(-qarg) / ksq
    frame_ref[...] = jnp.concatenate(
        [1.0 + sign * nx * nx * a, sign * b, -sign * nx, b, sign + ny * ny * a, -ny, factor, jnp.zeros_like(b)], axis=0
    )
    head = jnp.concatenate([m, m, m, jnp.zeros((HEAD - 9, kwaves), f32)], axis=0)
    wt_ref[...] = jnp.transpose(head).astype(bf16)


def trig(w, phase, tab_ref, rows, cols):
    u = jnp.dot(w, phase, preferred_element_type=f32)
    r = u - ((u + ROUND) - ROUND)
    s = r * horner(SIN, r * r)
    square = s * s
    tab_ref[0, rows, cols] = (1.0 - square).astype(bf16)
    rest = jnp.maximum(2.0 - square, TINY)
    tab_ref[1, rows, cols] = (s * (rest * lax.rsqrt(rest))).astype(bf16)


def trig_kernel(first, wt_ref, pack_ref, tab_ref):
    strip = 64
    phase = pack_ref[:HEAD]

    for row in range(0, tab_ref.shape[1], strip):
        trig(wt_ref[first + row : first + row + strip, :], phase, tab_ref, slice(row, row + strip), slice(None))


def unpacked(refs):
    blocks = []
    for ref in refs:
        blocks.extend([ref[...]] if len(ref.shape) == 2 else [ref[j] for j in range(ref.shape[0])])
    return blocks


def sums_kernel(first, offsets, chunk, frame_ref, wt_ref, *refs):
    count = len(offsets)
    ready, packs, todo = refs[:count], refs[count : 2 * count], refs[2 * count : -3]
    tab_ref, acc_ref, send_ref = refs[-3:]
    kwaves = tab_ref.shape[1]
    probes = acc_ref.shape[0] // 4
    blocks = unpacked(todo)
    width = blocks[0].shape[1]
    forces = jnp.concatenate([b[HEAD:] for b in blocks], axis=1)
    strip = 32

    sources = list(zip(ready, offsets, [pack[HEAD:] for pack in packs])) + [(tab_ref, 0, forces)]

    def sum_up(base, part):
        sums = 0.0
        for table, offset, force in sources:
            t = table[part, offset + base : offset + base + chunk, :]
            sums += lax.dot_general(force, t, (((1,), (1,)), ((), ())), preferred_element_type=f32)
        cols = slice(base, base + chunk)
        fr = frame_ref[:, first + base : first + base + chunk]
        for j in range(2):
            value = sum(fr[3 * j + x : 3 * j + x + 1] * sums[x * probes : (x + 1) * probes] for x in range(3))
            low = (2 * part + j) * probes
            acc_ref[low : low + probes, cols] = value
            send_ref[low : low + probes, cols] = value.astype(bf16)

    waiting = []
    for base in range(0, kwaves, chunk):
        for row in range(base, base + chunk, strip):
            w = wt_ref[first + row : first + row + strip, :]
            for j, block in enumerate(blocks):
                trig(w, block[:HEAD], tab_ref, slice(row, row + strip), slice(j * width, (j + 1) * width))
            if waiting and (row - base) // strip % PACE == 0:
                sum_up(*waiting.pop(0))
        waiting.extend((base, part) for part in range(2))
    for late in waiting:
        sum_up(*late)


def back_kernel(first, offsets, chunk, last, acc_ref, recv_ref, frame_ref, *refs):
    tables = refs[: len(offsets)]
    rest = refs[len(offsets) :]
    kwaves = acc_ref.shape[1]
    probes = acc_ref.shape[0] // 4
    halves = []
    for part in range(2):
        cols = slice(first, first + kwaves)
        t0, t1 = (
            frame_ref[6:7, cols] * (acc_ref[low : low + probes] + recv_ref[low : low + probes].astype(f32))
            for low in (2 * part * probes, (2 * part + 1) * probes)
        )
        halves.append(
            jnp.concatenate([frame_ref[x : x + 1, cols] * t0 + frame_ref[3 + x : 4 + x, cols] * t1 for x in range(3)], axis=0).astype(bf16)
        )
    begin = 0
    for offset, table in zip(offsets, tables):
        width = table.shape[2]
        total = sum(
            jnp.dot(halves[part], table[part, offset : offset + kwaves, :], preferred_element_type=f32) for part in range(2)
        )
        if not last:
            rest[0][:, begin : begin + width] = total
            begin += width
            continue
        earlier, keep, send = rest
        total += earlier[:, begin : begin + width]
        split = keep.shape[1]
        if begin < split:
            keep[:, begin : min(begin + width, split)] = total[:, : split - begin]
        if begin + width > split:
            low = max(begin, split)
            send[:, low - split : begin + width - split] = total[:, low - begin :].astype(bf16)
        begin += width


def shards(positions, forces, waves):
    wide, narrow = lax.axis_size("wide"), lax.axis_size("narrow")
    devices = wide * narrow
    bits = devices.bit_length() - 1
    assert devices == 1 << bits and bits >= 2
    rows = positions.shape[1]
    kwaves = waves.shape[1]
    half = forces.shape[0] * forces.shape[1]
    probes = forces.shape[1]
    top = devices >> 1
    amp = 20000.0 / float(rows * devices * kwaves) ** 0.5

    def swap(x, bit):
        return lax.ppermute(x, AXES, [(d, d ^ bit) for d in range(devices)])

    me = lax.axis_index(AXES)
    block = 2 * (me // top) + me % 2
    mine = kwaves // 4
    fl = 4 * half * rows
    shape = jax.ShapeDtypeStruct
    own, owned = call(
        pack_kernel,
        (shape((HEAD + half, rows), bf16), shape((3, mine), jnp.int32)),
        "pack",
        "shhh",
        scratch=[VMEM(positions.shape, f32), VMEM(forces.shape, f32), pltpu.SemaphoreType.DMA((3,))],
    )(block.reshape(1), *(pltpu.with_memory_space_constraint(x, pltpu.HBM) for x in (positions, forces, waves)))
    far = swap(own, top)
    frame, wt = call(
        functools.partial(frame_kernel, amp), (shape((8, mine), f32), shape((mine, HEAD), bf16)), "frame", "v", flops=mine * 1000
    )(owned)
    tab_own = call(functools.partial(trig_kernel, 0), shape((2, mine, rows), bf16), "trig_own", "vv", flops=mine * fl)(wt, own)
    both, tab_own, frame, wt = lax.optimization_barrier((jnp.stack([own, far]), tab_own, frame, wt))
    near = swap(both, 1)
    split = mine * 5 // 8 // 256 * 256
    parts = (split, mine - split)

    def trig_call(name, first, count, pack):
        return call(functools.partial(trig_kernel, first), shape((2, count, rows), bf16), name, "vv", flops=count * fl)(wt, pack)

    def sums(first, count, offsets, ready, packs, todo, width):
        return call(
            functools.partial(sums_kernel, first, offsets, 256),
            (shape((2, count, width), bf16), shape((4 * probes, count), f32), shape((4 * probes, count), bf16)),
            "sums",
            "v" * (2 + 2 * len(ready) + len(todo)),
            flops=count * fl * (width // rows),
        )(frame, wt, *ready, *packs, *todo)

    middle = [1 << j for j in range(1, bits - 1)]
    steps = len(middle)

    def exchange(x, j, chunk):
        turn = [middle[(j + core + 2 * chunk) % steps] for core in range(2)]
        return lax.ppermute(x, AXES, [(d, d ^ turn[d % 2]) for d in range(devices)])

    tab_far = trig_call("trig_far", 0, split, far)
    tab_a, acc_a, send_a = sums(0, parts[0], (0, 0), (tab_own, tab_far), (own, far), (near,), 2 * rows)
    tab_b, acc_b, send_b = sums(split, parts[1], (split,), (tab_own,), (own,), (far, near), 3 * rows)
    state = [[acc_a, send_a, None], [acc_b, send_b, None]]
    for j in range(steps):
        for chunk in range(2):
            acc, send, _ = state[chunk]
            got = exchange(send, j, chunk)
            if j + 1 < steps:
                acc = acc + got.astype(f32)
                send = acc.astype(bf16)
            state[chunk] = [acc, send, got]
    first = call(
        functools.partial(back_kernel, 0, (0, 0, 0), 256, False), shape((half, 4 * rows), f32), "back", "vvvvvv", flops=parts[0] * fl * 4
    )(state[0][0], state[0][2], frame, tab_own, tab_far, tab_a)
    keep, send = call(
        functools.partial(back_kernel, split, (split, 0), 256, True),
        (shape((half, 2 * rows), f32), shape((half, 2 * rows), bf16)),
        "back",
        "vvvvvv",
        flops=parts[1] * fl * 4,
    )(state[1][0], state[1][2], frame, tab_own, tab_b, first)
    there = swap(send, 1)
    keep = keep + there.astype(f32)
    there = swap(keep[:, rows:].astype(bf16), top)
    total = keep[:, :rows] + there.astype(f32)
    return total.reshape(forces.shape)


def solution(mesh):
    placed = (P(None, AXES), P(None, None, AXES), P())
    return jax.shard_map(
        shards,
        mesh=mesh,
        in_specs=placed,
        out_specs=P(None, None, AXES),
        check_vma=False,
    )
```

```python
import functools

import jax
import jax.numpy as jnp
from jax import lax
from jax.experimental import pallas as pl
from jax.experimental.pallas import tpu as pltpu
from jax.sharding import PartitionSpec as P

two_pi = 6.283185307179586
radius = 0.005
xi_split = 40.0
AXES = ("wide", "narrow")
VMEM = pltpu.VMEM
SMEM = pltpu.SMEM
f32, bf16 = jnp.float32, jnp.bfloat16

SIN = (4.442867901617319, -7.307443368323551, 3.594787581869042, -0.7843727161608242)
ROUND = 12582912.0
TINY = 1e-30
PACE = 2
HEAD = 16


def horner(coeffs, q):
    total = coeffs[-1] * q + coeffs[-2]
    for c in reversed(coeffs[:-2]):
        total = total * q + c
    return total


def call(kernel, out_shape, name, specs, scratch=(), flops=0):
    many = isinstance(out_shape, (list, tuple))
    spaces = {"v": VMEM, "s": SMEM, "h": pltpu.HBM}
    return pl.pallas_call(
        kernel,
        out_shape=out_shape,
        in_specs=[pl.BlockSpec(memory_space=spaces[x]) for x in specs],
        out_specs=[pl.BlockSpec(memory_space=VMEM)] * len(out_shape) if many else pl.BlockSpec(memory_space=VMEM),
        scratch_shapes=scratch,
        name=name,
        compiler_params=pltpu.CompilerParams(vmem_limit_bytes=24 << 20),
        cost_estimate=pl.CostEstimate(flops=flops, bytes_accessed=flops // 256, transcendentals=0),
    )


def split3(x):
    hi = x.astype(bf16)
    rest = x - hi.astype(f32)
    mid = rest.astype(bf16)
    low = (rest - mid.astype(f32)).astype(bf16)
    return hi, mid, low


def pack_kernel(idx_ref, pos_hbm, force_hbm, waves_hbm, out_ref, own_ref, pos_ref, force_ref, sems):
    first = pl.multiple_of(idx_ref[0] * own_ref.shape[1], 128)
    copies = [
        pltpu.make_async_copy(pos_hbm, pos_ref, sems.at[0]),
        pltpu.make_async_copy(force_hbm, force_ref, sems.at[1]),
        pltpu.make_async_copy(waves_hbm.at[:, pl.ds(first, own_ref.shape[1])], own_ref, sems.at[2]),
    ]
    for copy in copies:
        copy.start()
    for copy in copies:
        copy.wait()
    hi, mid, low = split3(pos_ref[...])
    rows = out_ref.shape[1]
    parts = [hi.astype(f32), mid.astype(f32), low.astype(f32), jnp.zeros((HEAD - 9, rows), f32)]
    out_ref[:HEAD, :] = jnp.concatenate(parts, axis=0).astype(bf16)
    for a in range(force_ref.shape[0]):
        p = force_ref.shape[1]
        out_ref[HEAD + a * p : HEAD + (a + 1) * p, :] = force_ref[a].astype(bf16)


def frame_kernel(amp, own_ref, frame_ref, wt_ref):
    kwaves = own_ref.shape[1]
    m = own_ref[...].astype(f32)
    msq = jnp.sum(m * m, axis=0, keepdims=True)
    n = m * lax.rsqrt(msq)
    nx, ny, nz = n[0:1], n[1:2], n[2:3]
    sign = jnp.where(nz >= 0.0, 1.0, -1.0)
    a = -1.0 / (sign + nz)
    b = nx * ny * a
    ksq = (two_pi * two_pi) * msq
    qarg = ksq / (4.0 * xi_split * xi_split)
    factor = amp * (1.0 - radius * radius * ksq / 3.0) * (1.0 + qarg + 2.0 * qarg * qarg) * jnp.exp(-qarg) / ksq
    frame_ref[...] = jnp.concatenate(
        [1.0 + sign * nx * nx * a, sign * b, -sign * nx, b, sign + ny * ny * a, -ny, factor, jnp.zeros_like(b)], axis=0
    )
    head = jnp.concatenate([m, m, m, jnp.zeros((HEAD - 9, kwaves), f32)], axis=0)
    wt_ref[...] = jnp.transpose(head).astype(bf16)


def trig(w, phase, tab_ref, rows, cols):
    u = jnp.dot(w, phase, preferred_element_type=f32)
    r = u - ((u + ROUND) - ROUND)
    s = r * horner(SIN, r * r)
    square = s * s
    tab_ref[0, rows, cols] = (1.0 - square).astype(bf16)
    rest = jnp.maximum(2.0 - square, TINY)
    tab_ref[1, rows, cols] = (s * (rest * lax.rsqrt(rest))).astype(bf16)


def product(force, table):
    return lax.dot_general(force, table, (((1,), (1,)), ((), ())), preferred_element_type=f32)


def trig_kernel(first, chunk, wt_ref, pack_ref, *refs):
    earlier, tab_ref, raw_ref = refs if len(refs) == 3 else (None, *refs)
    half = pack_ref.shape[0] - HEAD
    strip = 64
    phase, force = pack_ref[:HEAD], pack_ref[HEAD:]
    count = tab_ref.shape[1]

    def sum_up(base, part):
        rows, cols = slice(part * half, (part + 1) * half), slice(base, base + chunk)
        sums = product(force, tab_ref[part, cols, :])
        raw_ref[rows, cols] = sums if earlier is None else sums + earlier[rows, cols]

    waiting = []
    for base in range(0, count, chunk):
        for row in range(base, base + chunk, strip):
            trig(wt_ref[first + row : first + row + strip, :], phase, tab_ref, slice(row, row + strip), slice(None))
            if waiting and (row - base) // strip % 2 == 0:
                sum_up(*waiting.pop(0))
        waiting.extend((base, part) for part in range(2))
    for late in waiting:
        sum_up(*late)


def unpacked(refs):
    blocks = []
    for ref in refs:
        blocks.extend([ref[...]] if len(ref.shape) == 2 else [ref[j] for j in range(ref.shape[0])])
    return blocks


def sums_kernel(first, start, chunk, frame_ref, wt_ref, raw_ref, *refs):
    todo = refs[:-3]
    tab_ref, acc_ref, send_ref = refs[-3:]
    kwaves = tab_ref.shape[1]
    probes = acc_ref.shape[0] // 4
    half = 3 * probes
    blocks = unpacked(todo)
    width = blocks[0].shape[1]
    forces = jnp.concatenate([b[HEAD:] for b in blocks], axis=1)
    strip = 32

    def sum_up(base, part):
        cols = slice(base, base + chunk)
        sums = product(forces, tab_ref[part, cols, :]) + raw_ref[part * half : (part + 1) * half, start + base : start + base + chunk]
        fr = frame_ref[:, first + base : first + base + chunk]
        for j in range(2):
            value = sum(fr[3 * j + x : 3 * j + x + 1] * sums[x * probes : (x + 1) * probes] for x in range(3))
            low = (2 * part + j) * probes
            acc_ref[low : low + probes, cols] = value
            send_ref[low : low + probes, cols] = value.astype(bf16)

    waiting = []
    for base in range(0, kwaves, chunk):
        for row in range(base, base + chunk, strip):
            w = wt_ref[first + row : first + row + strip, :]
            for j, block in enumerate(blocks):
                trig(w, block[:HEAD], tab_ref, slice(row, row + strip), slice(j * width, (j + 1) * width))
            if waiting and (row - base) // strip % PACE == 0:
                sum_up(*waiting.pop(0))
        waiting.extend((base, part) for part in range(2))
    for late in waiting:
        sum_up(*late)


def back_kernel(first, offsets, chunk, last, acc_ref, recv_ref, frame_ref, *refs):
    tables = refs[: len(offsets)]
    rest = refs[len(offsets) :]
    kwaves = acc_ref.shape[1]
    probes = acc_ref.shape[0] // 4
    halves = []
    for part in range(2):
        cols = slice(first, first + kwaves)
        t0, t1 = (
            frame_ref[6:7, cols] * (acc_ref[low : low + probes] + recv_ref[low : low + probes].astype(f32))
            for low in (2 * part * probes, (2 * part + 1) * probes)
        )
        halves.append(
            jnp.concatenate([frame_ref[x : x + 1, cols] * t0 + frame_ref[3 + x : 4 + x, cols] * t1 for x in range(3)], axis=0).astype(bf16)
        )
    begin = 0
    for offset, table in zip(offsets, tables):
        width = table.shape[2]
        total = sum(
            jnp.dot(halves[part], table[part, offset : offset + kwaves, :], preferred_element_type=f32) for part in range(2)
        )
        if not last:
            rest[0][:, begin : begin + width] = total
            begin += width
            continue
        earlier, keep, send = rest
        total += earlier[:, begin : begin + width]
        split = keep.shape[1]
        if begin < split:
            keep[:, begin : min(begin + width, split)] = total[:, : split - begin]
        if begin + width > split:
            low = max(begin, split)
            send[:, low - split : begin + width - split] = total[:, low - begin :].astype(bf16)
        begin += width


def shards(positions, forces, waves):
    wide, narrow = lax.axis_size("wide"), lax.axis_size("narrow")
    devices = wide * narrow
    bits = devices.bit_length() - 1
    assert devices == 1 << bits and bits >= 2
    rows = positions.shape[1]
    kwaves = waves.shape[1]
    half = forces.shape[0] * forces.shape[1]
    probes = forces.shape[1]
    top = devices >> 1
    amp = 20000.0 / float(rows * devices * kwaves) ** 0.5

    def swap(x, bit):
        return lax.ppermute(x, AXES, [(d, d ^ bit) for d in range(devices)])

    me = lax.axis_index(AXES)
    block = 2 * (me // top) + me % 2
    mine = kwaves // 4
    fl = 4 * half * rows
    shape = jax.ShapeDtypeStruct
    own, owned = call(
        pack_kernel,
        (shape((HEAD + half, rows), bf16), shape((3, mine), jnp.int32)),
        "pack",
        "shhh",
        scratch=[VMEM(positions.shape, f32), VMEM(forces.shape, f32), pltpu.SemaphoreType.DMA((3,))],
    )(block.reshape(1), *(pltpu.with_memory_space_constraint(x, pltpu.HBM) for x in (positions, forces, waves)))
    far = swap(own, top)
    frame, wt = call(
        functools.partial(frame_kernel, amp), (shape((8, mine), f32), shape((mine, HEAD), bf16)), "frame", "v", flops=mine * 1000
    )(owned)

    def trig_call(name, first, count, *operands):
        return call(
            functools.partial(trig_kernel, first, 256),
            (shape((2, count, rows), bf16), shape((2 * half, count), f32)),
            name,
            "v" * (1 + len(operands)),
            flops=count * fl,
        )(wt, *operands)

    tab_own, raw = trig_call("trig_own", 0, mine, own)
    both, tab_own, raw, frame, wt = lax.optimization_barrier((jnp.stack([own, far]), tab_own, raw, frame, wt))
    near = swap(both, 1)
    split = mine * 5 // 8 // 256 * 256
    parts = (split, mine - split)

    def sums(first, count, start, raw, todo, width):
        return call(
            functools.partial(sums_kernel, first, start, 256),
            (shape((2, count, width), bf16), shape((4 * probes, count), f32), shape((4 * probes, count), bf16)),
            "sums",
            "v" * (3 + len(todo)),
            flops=count * fl * (width // rows),
        )(frame, wt, raw, *todo)

    middle = [1 << j for j in range(1, bits - 1)]
    steps = len(middle)

    def exchange(x, j, chunk):
        turn = [middle[(j + core + 2 * chunk) % steps] for core in range(2)]
        return lax.ppermute(x, AXES, [(d, d ^ turn[d % 2]) for d in range(devices)])

    tab_far, raw_a = trig_call("trig_far", 0, split, far, raw)
    tab_a, acc_a, send_a = sums(0, parts[0], 0, raw_a, (near,), 2 * rows)
    tab_b, acc_b, send_b = sums(split, parts[1], split, raw, (far, near), 3 * rows)
    state = [[acc_a, send_a, None], [acc_b, send_b, None]]
    for j in range(steps):
        for chunk in range(2):
            acc, send, _ = state[chunk]
            got = exchange(send, j, chunk)
            if j + 1 < steps:
                acc = acc + got.astype(f32)
                send = acc.astype(bf16)
            state[chunk] = [acc, send, got]
    first = call(
        functools.partial(back_kernel, 0, (0, 0, 0), 256, False), shape((half, 4 * rows), f32), "back", "vvvvvv", flops=parts[0] * fl * 4
    )(state[0][0], state[0][2], frame, tab_own, tab_far, tab_a)
    keep, send = call(
        functools.partial(back_kernel, split, (split, 0), 256, True),
        (shape((half, 2 * rows), f32), shape((half, 2 * rows), bf16)),
        "back",
        "vvvvvv",
        flops=parts[1] * fl * 4,
    )(state[1][0], state[1][2], frame, tab_own, tab_b, first)
    there = swap(send, 1)
    keep = keep + there.astype(f32)
    there = swap(keep[:, rows:].astype(bf16), top)
    total = keep[:, :rows] + there.astype(f32)
    return total.reshape(forces.shape)


def solution(mesh):
    placed = (P(None, AXES), P(None, None, AXES), P())
    return jax.shard_map(
        shards,
        mesh=mesh,
        in_specs=placed,
        out_specs=P(None, None, AXES),
        check_vma=False,
    )
```

```python
import functools

import jax
import jax.numpy as jnp
from jax import lax
from jax.experimental import pallas as pl
from jax.experimental.pallas import tpu as pltpu
from jax.sharding import PartitionSpec as P

two_pi = 6.283185307179586
radius = 0.005
xi_split = 40.0
AXES = ("wide", "narrow")
VMEM = pltpu.VMEM
SMEM = pltpu.SMEM
f32, bf16 = jnp.float32, jnp.bfloat16

SIN = (4.442867901617319, -7.307443368323551, 3.594787581869042, -0.7843727161608242)
TINY = 1e-30
STRIP = 32
PACE = 2
HEAD = 16


def horner(coeffs, q):
    total = coeffs[-1] * q + coeffs[-2]
    for c in reversed(coeffs[:-2]):
        total = total * q + c
    return total


def call(kernel, out_shape, name, specs, scratch=(), flops=0):
    many = isinstance(out_shape, (list, tuple))
    spaces = {"v": VMEM, "s": SMEM, "h": pltpu.HBM}
    return pl.pallas_call(
        kernel,
        out_shape=out_shape,
        in_specs=[pl.BlockSpec(memory_space=spaces[x]) for x in specs],
        out_specs=[pl.BlockSpec(memory_space=VMEM)] * len(out_shape) if many else pl.BlockSpec(memory_space=VMEM),
        scratch_shapes=scratch,
        name=name,
        compiler_params=pltpu.CompilerParams(vmem_limit_bytes=24 << 20),
        cost_estimate=pl.CostEstimate(flops=flops, bytes_accessed=flops // 256, transcendentals=0),
    )


def split3(x):
    hi = x.astype(bf16)
    rest = x - hi.astype(f32)
    mid = rest.astype(bf16)
    low = (rest - mid.astype(f32)).astype(bf16)
    return hi, mid, low


def pack_kernel(idx_ref, pos_hbm, force_hbm, waves_hbm, out_ref, own_ref, pos_ref, force_ref, sems):
    first = pl.multiple_of(idx_ref[0] * own_ref.shape[1], 128)
    copies = [
        pltpu.make_async_copy(pos_hbm, pos_ref, sems.at[0]),
        pltpu.make_async_copy(force_hbm, force_ref, sems.at[1]),
        pltpu.make_async_copy(waves_hbm.at[:, pl.ds(first, own_ref.shape[1])], own_ref, sems.at[2]),
    ]
    for copy in copies:
        copy.start()
    for copy in copies:
        copy.wait()
    hi, mid, low = split3(pos_ref[...])
    rows = out_ref.shape[1]
    parts = [hi.astype(f32), mid.astype(f32), low.astype(f32), jnp.zeros((HEAD - 9, rows), f32)]
    out_ref[:HEAD, :] = jnp.concatenate(parts, axis=0).astype(bf16)
    for a in range(force_ref.shape[0]):
        p = force_ref.shape[1]
        out_ref[HEAD + a * p : HEAD + (a + 1) * p, :] = force_ref[a].astype(bf16)


def frame_kernel(amp, own_ref, frame_ref, wt_ref):
    kwaves = own_ref.shape[1]
    m = own_ref[...].astype(f32)
    msq = jnp.sum(m * m, axis=0, keepdims=True)
    n = m * lax.rsqrt(msq)
    nx, ny, nz = n[0:1], n[1:2], n[2:3]
    sign = jnp.where(nz >= 0.0, 1.0, -1.0)
    a = -1.0 / (sign + nz)
    b = nx * ny * a
    ksq = (two_pi * two_pi) * msq
    qarg = ksq / (4.0 * xi_split * xi_split)
    factor = amp * (1.0 - radius * radius * ksq / 3.0) * (1.0 + qarg + 2.0 * qarg * qarg) * jnp.exp(-qarg) / ksq
    frame_ref[...] = jnp.concatenate(
        [1.0 + sign * nx * nx * a, sign * b, -sign * nx, b, sign + ny * ny * a, -ny, factor, jnp.zeros_like(b)], axis=0
    )
    head = jnp.concatenate([m, m, m, jnp.zeros((HEAD - 9, kwaves), f32)], axis=0)
    wt_ref[...] = jnp.transpose(head).astype(bf16)


def trig(u, tab_ref, rows, cols):
    r = u - jnp.round(u)
    s = r * horner(SIN, r * r)
    square = s * s
    tab_ref[0, rows, cols] = (1.0 - square).astype(bf16)
    rest = jnp.maximum(2.0 - square, TINY)
    tab_ref[1, rows, cols] = (s * (rest * lax.rsqrt(rest))).astype(bf16)


def tables(first, chunk, wt_ref, phase, tab_ref, u_ref, sum_up):
    count = tab_ref.shape[1]
    width = phase.shape[1]
    lanes = min(width, 256)

    def phases(base):
        w = wt_ref[first + base : first + base + chunk, :]
        u_ref[base // chunk % 2] = jnp.dot(w, phase, preferred_element_type=f32)

    phases(0)
    waiting = []
    for base in range(0, count, chunk):
        if base + chunk < count:
            phases(base + chunk)
        for row in range(0, chunk, STRIP):
            for low in range(0, width, lanes):
                cols = slice(low, low + lanes)
                trig(u_ref[base // chunk % 2, row : row + STRIP, cols], tab_ref, slice(base + row, base + row + STRIP), cols)
            if waiting and row // STRIP % PACE == 0:
                sum_up(*waiting.pop(0))
        waiting.extend((base, part) for part in range(2))
    for late in waiting:
        sum_up(*late)


def product(force, table):
    return lax.dot_general(force, table, (((1,), (1,)), ((), ())), preferred_element_type=f32)


def trig_kernel(first, chunk, wt_ref, pack_ref, *refs):
    earlier, tab_ref, raw_ref, u_ref = refs if len(refs) == 4 else (None, *refs)
    half = pack_ref.shape[0] - HEAD
    phase, force = pack_ref[:HEAD], pack_ref[HEAD:]

    def sum_up(base, part):
        rows, cols = slice(part * half, (part + 1) * half), slice(base, base + chunk)
        sums = product(force, tab_ref[part, cols, :])
        raw_ref[rows, cols] = sums if earlier is None else sums + earlier[rows, cols]

    tables(first, chunk, wt_ref, phase, tab_ref, u_ref, sum_up)


def unpacked(refs):
    blocks = []
    for ref in refs:
        blocks.extend([ref[...]] if len(ref.shape) == 2 else [ref[j] for j in range(ref.shape[0])])
    return blocks


def sums_kernel(first, start, chunk, frame_ref, wt_ref, raw_ref, *refs):
    todo = refs[:-4]
    tab_ref, acc_ref, send_ref, u_ref = refs[-4:]
    kwaves = tab_ref.shape[1]
    probes = acc_ref.shape[0] // 4
    half = 3 * probes
    blocks = unpacked(todo)
    phase = jnp.concatenate([b[:HEAD] for b in blocks], axis=1)
    forces = jnp.concatenate([b[HEAD:] for b in blocks], axis=1)

    def sum_up(base, part):
        cols = slice(base, base + chunk)
        sums = product(forces, tab_ref[part, cols, :]) + raw_ref[part * half : (part + 1) * half, start + base : start + base + chunk]
        fr = frame_ref[:, first + base : first + base + chunk]
        for j in range(2):
            value = sum(fr[3 * j + x : 3 * j + x + 1] * sums[x * probes : (x + 1) * probes] for x in range(3))
            low = (2 * part + j) * probes
            acc_ref[low : low + probes, cols] = value
            send_ref[low : low + probes, cols] = value.astype(bf16)

    tables(first, chunk, wt_ref, phase, tab_ref, u_ref, sum_up)


def back_kernel(first, offsets, chunk, last, acc_ref, recv_ref, frame_ref, *refs):
    tables = refs[: len(offsets)]
    rest = refs[len(offsets) :]
    kwaves = acc_ref.shape[1]
    probes = acc_ref.shape[0] // 4
    halves = []
    for part in range(2):
        cols = slice(first, first + kwaves)
        t0, t1 = (
            frame_ref[6:7, cols] * (acc_ref[low : low + probes] + recv_ref[low : low + probes].astype(f32))
            for low in (2 * part * probes, (2 * part + 1) * probes)
        )
        halves.append(
            jnp.concatenate([frame_ref[x : x + 1, cols] * t0 + frame_ref[3 + x : 4 + x, cols] * t1 for x in range(3)], axis=0).astype(bf16)
        )
    begin = 0
    for offset, table in zip(offsets, tables):
        width = table.shape[2]
        total = sum(
            jnp.dot(halves[part], table[part, offset : offset + kwaves, :], preferred_element_type=f32) for part in range(2)
        )
        if not last:
            rest[0][:, begin : begin + width] = total
            begin += width
            continue
        earlier, keep, send = rest
        total += earlier[:, begin : begin + width]
        split = keep.shape[1]
        if begin < split:
            keep[:, begin : min(begin + width, split)] = total[:, : split - begin]
        if begin + width > split:
            low = max(begin, split)
            send[:, low - split : begin + width - split] = total[:, low - begin :].astype(bf16)
        begin += width


def shards(positions, forces, waves):
    wide, narrow = lax.axis_size("wide"), lax.axis_size("narrow")
    devices = wide * narrow
    bits = devices.bit_length() - 1
    assert devices == 1 << bits and bits >= 2
    rows = positions.shape[1]
    kwaves = waves.shape[1]
    half = forces.shape[0] * forces.shape[1]
    probes = forces.shape[1]
    top = devices >> 1
    amp = 20000.0 / float(rows * devices * kwaves) ** 0.5

    def swap(x, bit):
        return lax.ppermute(x, AXES, [(d, d ^ bit) for d in range(devices)])

    me = lax.axis_index(AXES)
    block = 2 * (me // top) + me % 2
    mine = kwaves // 4
    fl = 4 * half * rows
    shape = jax.ShapeDtypeStruct
    own, owned = call(
        pack_kernel,
        (shape((HEAD + half, rows), bf16), shape((3, mine), jnp.int32)),
        "pack",
        "shhh",
        scratch=[VMEM(positions.shape, f32), VMEM(forces.shape, f32), pltpu.SemaphoreType.DMA((3,))],
    )(block.reshape(1), *(pltpu.with_memory_space_constraint(x, pltpu.HBM) for x in (positions, forces, waves)))
    far = swap(own, top)
    frame, wt = call(
        functools.partial(frame_kernel, amp), (shape((8, mine), f32), shape((mine, HEAD), bf16)), "frame", "v", flops=mine * 1000
    )(owned)

    def trig_call(name, first, count, *operands):
        return call(
            functools.partial(trig_kernel, first, 256),
            (shape((2, count, rows), bf16), shape((2 * half, count), f32)),
            name,
            "v" * (1 + len(operands)),
            scratch=[VMEM((2, 256, rows), f32)],
            flops=count * fl,
        )(wt, *operands)

    tab_own, raw = trig_call("trig_own", 0, mine, own)
    both, tab_own, raw, frame, wt = lax.optimization_barrier((jnp.stack([own, far]), tab_own, raw, frame, wt))
    near = swap(both, 1)
    split = mine * 5 // 8 // 256 * 256
    parts = (split, mine - split)

    def sums(first, count, start, raw, todo, width):
        return call(
            functools.partial(sums_kernel, first, start, 256),
            (shape((2, count, width), bf16), shape((4 * probes, count), f32), shape((4 * probes, count), bf16)),
            "sums",
            "v" * (3 + len(todo)),
            scratch=[VMEM((2, 256, width), f32)],
            flops=count * fl * (width // rows),
        )(frame, wt, raw, *todo)

    middle = [1 << j for j in range(1, bits - 1)]
    steps = len(middle)

    def exchange(x, j, chunk):
        turn = [middle[(j + core + 2 * chunk) % steps] for core in range(2)]
        return lax.ppermute(x, AXES, [(d, d ^ turn[d % 2]) for d in range(devices)])

    tab_far, raw_a = trig_call("trig_far", 0, split, far, raw)
    tab_a, acc_a, send_a = sums(0, parts[0], 0, raw_a, (near,), 2 * rows)
    tab_b, acc_b, send_b = sums(split, parts[1], split, raw, (far, near), 3 * rows)
    state = [[acc_a, send_a, None], [acc_b, send_b, None]]
    for j in range(steps):
        for chunk in range(2):
            acc, send, _ = state[chunk]
            got = exchange(send, j, chunk)
            if j + 1 < steps:
                acc = acc + got.astype(f32)
                send = acc.astype(bf16)
            state[chunk] = [acc, send, got]
    first = call(
        functools.partial(back_kernel, 0, (0, 0, 0), 256, False), shape((half, 4 * rows), f32), "back", "vvvvvv", flops=parts[0] * fl * 4
    )(state[0][0], state[0][2], frame, tab_own, tab_far, tab_a)
    keep, send = call(
        functools.partial(back_kernel, split, (split, 0), 256, True),
        (shape((half, 2 * rows), f32), shape((half, 2 * rows), bf16)),
        "back",
        "vvvvvv",
        flops=parts[1] * fl * 4,
    )(state[1][0], state[1][2], frame, tab_own, tab_b, first)
    there = swap(send, 1)
    keep = keep + there.astype(f32)
    there = swap(keep[:, rows:].astype(bf16), top)
    total = keep[:, :rows] + there.astype(f32)
    return total.reshape(forces.shape)


def solution(mesh):
    placed = (P(None, AXES), P(None, None, AXES), P())
    return jax.shard_map(
        shards,
        mesh=mesh,
        in_specs=placed,
        out_specs=P(None, None, AXES),
        check_vma=False,
    )
```

```python
import functools

import jax
import jax.numpy as jnp
from jax import lax
from jax.experimental import pallas as pl
from jax.experimental.pallas import tpu as pltpu
from jax.sharding import PartitionSpec as P

two_pi = 6.283185307179586
radius = 0.005
xi_split = 40.0
AXES = ("wide", "narrow")
VMEM = pltpu.VMEM
SMEM = pltpu.SMEM
f32, bf16 = jnp.float32, jnp.bfloat16

SIN = (4.4428676475109, -7.307433203747474, 3.5946900772135946, -0.7841130155066478)
STRIP = 32
PACE = 2
HEAD = 16


def horner(coeffs, q):
    total = coeffs[-1] * q + coeffs[-2]
    for c in reversed(coeffs[:-2]):
        total = total * q + c
    return total


def call(kernel, out_shape, name, specs, scratch=(), flops=0):
    many = isinstance(out_shape, (list, tuple))
    spaces = {"v": VMEM, "s": SMEM, "h": pltpu.HBM}
    return pl.pallas_call(
        kernel,
        out_shape=out_shape,
        in_specs=[pl.BlockSpec(memory_space=spaces[x]) for x in specs],
        out_specs=[pl.BlockSpec(memory_space=VMEM)] * len(out_shape) if many else pl.BlockSpec(memory_space=VMEM),
        scratch_shapes=scratch,
        name=name,
        compiler_params=pltpu.CompilerParams(vmem_limit_bytes=24 << 20),
        cost_estimate=pl.CostEstimate(flops=flops, bytes_accessed=flops // 256, transcendentals=0),
    )


def split3(x):
    hi = x.astype(bf16)
    rest = x - hi.astype(f32)
    mid = rest.astype(bf16)
    low = (rest - mid.astype(f32)).astype(bf16)
    return hi, mid, low


def pack_kernel(idx_ref, pos_hbm, force_hbm, waves_hbm, out_ref, own_ref, pos_ref, force_ref, sems):
    first = pl.multiple_of(idx_ref[0] * own_ref.shape[1], 128)
    copies = [
        pltpu.make_async_copy(pos_hbm, pos_ref, sems.at[0]),
        pltpu.make_async_copy(force_hbm, force_ref, sems.at[1]),
        pltpu.make_async_copy(waves_hbm.at[:, pl.ds(first, own_ref.shape[1])], own_ref, sems.at[2]),
    ]
    for copy in copies:
        copy.start()
    for copy in copies:
        copy.wait()
    hi, mid, low = split3(pos_ref[...])
    rows = out_ref.shape[1]
    parts = [hi.astype(f32), mid.astype(f32), low.astype(f32), jnp.zeros((HEAD - 9, rows), f32)]
    out_ref[:HEAD, :] = jnp.concatenate(parts, axis=0).astype(bf16)
    for a in range(force_ref.shape[0]):
        p = force_ref.shape[1]
        out_ref[HEAD + a * p : HEAD + (a + 1) * p, :] = force_ref[a].astype(bf16)


def frame_kernel(amp, own_ref, frame_ref, wt_ref):
    kwaves = own_ref.shape[1]
    m = own_ref[...].astype(f32)
    msq = jnp.sum(m * m, axis=0, keepdims=True)
    n = m * lax.rsqrt(msq)
    nx, ny, nz = n[0:1], n[1:2], n[2:3]
    sign = jnp.where(nz >= 0.0, 1.0, -1.0)
    a = -1.0 / (sign + nz)
    b = nx * ny * a
    ksq = (two_pi * two_pi) * msq
    qarg = ksq / (4.0 * xi_split * xi_split)
    factor = amp * (1.0 - radius * radius * ksq / 3.0) * (1.0 + qarg + 2.0 * qarg * qarg) * jnp.exp(-qarg) / ksq
    frame_ref[...] = jnp.concatenate(
        [1.0 + sign * nx * nx * a, sign * b, -sign * nx, b, sign + ny * ny * a, -ny, factor, jnp.zeros_like(b)], axis=0
    )
    head = jnp.concatenate([m, m, m, jnp.zeros((HEAD - 9, kwaves), f32)], axis=0)
    wt_ref[...] = jnp.transpose(head).astype(bf16)


def trig(u, tab_ref, rows, cols):
    r = u - jnp.round(u)
    s = r * horner(SIN, r * r)
    square = s * s
    tab_ref[0, rows, cols] = (1.0 - square).astype(bf16)
    rest = 2.0 - square
    tab_ref[1, rows, cols] = (s * (rest * lax.rsqrt(rest))).astype(bf16)


def runs_of(count):
    cuts = [*range(0, count, 256), count] if count % 256 else [*range(0, count - 256, 256), count - 256, count - 128, count]
    return [(a, b - a) for a, b in zip(cuts, cuts[1:])]


def tables(first, wt_ref, phase, tab_ref, u_ref, sum_up):
    width = phase.shape[1]
    lanes = min(width, 256)
    runs = runs_of(tab_ref.shape[1])

    def phases(n):
        base, count = runs[n]
        w = wt_ref[first + base : first + base + count, :]
        u_ref[n % 2, :count] = jnp.dot(w, phase, preferred_element_type=f32)

    phases(0)
    waiting = []
    for n, (base, count) in enumerate(runs):
        if n + 1 < len(runs):
            phases(n + 1)
        for row in range(0, count, STRIP):
            for low in range(0, width, lanes):
                cols = slice(low, low + lanes)
                trig(u_ref[n % 2, row : row + STRIP, cols], tab_ref, slice(base + row, base + row + STRIP), cols)
            if waiting and row // STRIP % PACE == 0:
                sum_up(*waiting.pop(0))
        waiting.extend((slice(base, base + count), part) for part in range(2))
    for late in waiting:
        sum_up(*late)


def product(force, table):
    return lax.dot_general(force, table, (((1,), (1,)), ((), ())), preferred_element_type=f32)


def trig_kernel(first, wt_ref, pack_ref, *refs):
    earlier, tab_ref, raw_ref, u_ref = refs if len(refs) == 4 else (None, *refs)
    half = pack_ref.shape[0] - HEAD
    phase, force = pack_ref[:HEAD], pack_ref[HEAD:]

    def sum_up(cols, part):
        rows = slice(part * half, (part + 1) * half)
        sums = product(force, tab_ref[part, cols, :])
        raw_ref[rows, cols] = sums if earlier is None else sums + earlier[rows, cols]

    tables(first, wt_ref, phase, tab_ref, u_ref, sum_up)


def unpacked(refs):
    blocks = []
    for ref in refs:
        blocks.extend([ref[...]] if len(ref.shape) == 2 else [ref[j] for j in range(ref.shape[0])])
    return blocks


def sums_kernel(first, start, frame_ref, wt_ref, raw_ref, *refs):
    todo = refs[:-4]
    tab_ref, acc_ref, send_ref, u_ref = refs[-4:]
    kwaves = tab_ref.shape[1]
    probes = acc_ref.shape[0] // 4
    half = 3 * probes
    blocks = unpacked(todo)
    phase = jnp.concatenate([b[:HEAD] for b in blocks], axis=1)
    forces = jnp.concatenate([b[HEAD:] for b in blocks], axis=1)

    def sum_up(cols, part):
        sums = product(forces, tab_ref[part, cols, :]) + raw_ref[part * half : (part + 1) * half, start + cols.start : start + cols.stop]
        fr = frame_ref[:, first + cols.start : first + cols.stop]
        for j in range(2):
            value = sum(fr[3 * j + x : 3 * j + x + 1] * sums[x * probes : (x + 1) * probes] for x in range(3))
            low = (2 * part + j) * probes
            acc_ref[low : low + probes, cols] = value
            send_ref[low : low + probes, cols] = value.astype(bf16)

    tables(first, wt_ref, phase, tab_ref, u_ref, sum_up)


def back_kernel(first, offsets, chunk, last, acc_ref, recv_ref, frame_ref, *refs):
    tables = refs[: len(offsets)]
    rest = refs[len(offsets) :]
    kwaves = acc_ref.shape[1]
    probes = acc_ref.shape[0] // 4
    halves = []
    for part in range(2):
        cols = slice(first, first + kwaves)
        t0, t1 = (
            frame_ref[6:7, cols] * (acc_ref[low : low + probes] + recv_ref[low : low + probes].astype(f32))
            for low in (2 * part * probes, (2 * part + 1) * probes)
        )
        halves.append(
            jnp.concatenate([frame_ref[x : x + 1, cols] * t0 + frame_ref[3 + x : 4 + x, cols] * t1 for x in range(3)], axis=0).astype(bf16)
        )
    begin = 0
    for offset, table in zip(offsets, tables):
        width = table.shape[2]
        total = sum(
            jnp.dot(halves[part], table[part, offset : offset + kwaves, :], preferred_element_type=f32) for part in range(2)
        )
        if not last:
            rest[0][:, begin : begin + width] = total
            begin += width
            continue
        earlier, keep, send = rest
        total += earlier[:, begin : begin + width]
        split = keep.shape[1]
        if begin < split:
            keep[:, begin : min(begin + width, split)] = total[:, : split - begin]
        if begin + width > split:
            low = max(begin, split)
            send[:, low - split : begin + width - split] = total[:, low - begin :].astype(bf16)
        begin += width


def shards(positions, forces, waves):
    wide, narrow = lax.axis_size("wide"), lax.axis_size("narrow")
    devices = wide * narrow
    bits = devices.bit_length() - 1
    assert devices == 1 << bits and bits >= 2
    rows = positions.shape[1]
    kwaves = waves.shape[1]
    half = forces.shape[0] * forces.shape[1]
    probes = forces.shape[1]
    top = devices >> 1
    amp = 20000.0 / float(rows * devices * kwaves) ** 0.5

    def swap(x, bit):
        return lax.ppermute(x, AXES, [(d, d ^ bit) for d in range(devices)])

    me = lax.axis_index(AXES)
    block = 2 * (me // top) + me % 2
    mine = kwaves // 4
    fl = 4 * half * rows
    shape = jax.ShapeDtypeStruct
    own, owned = call(
        pack_kernel,
        (shape((HEAD + half, rows), bf16), shape((3, mine), jnp.int32)),
        "pack",
        "shhh",
        scratch=[VMEM(positions.shape, f32), VMEM(forces.shape, f32), pltpu.SemaphoreType.DMA((3,))],
    )(block.reshape(1), *(pltpu.with_memory_space_constraint(x, pltpu.HBM) for x in (positions, forces, waves)))
    far = swap(own, top)
    frame, wt = call(
        functools.partial(frame_kernel, amp), (shape((8, mine), f32), shape((mine, HEAD), bf16)), "frame", "v", flops=mine * 1000
    )(owned)

    def trig_call(name, first, count, *operands):
        return call(
            functools.partial(trig_kernel, first),
            (shape((2, count, rows), bf16), shape((2 * half, count), f32)),
            name,
            "v" * (1 + len(operands)),
            scratch=[VMEM((2, 256, rows), f32)],
            flops=count * fl,
        )(wt, *operands)

    tab_own, raw = trig_call("trig_own", 0, mine, own)
    both, tab_own, raw, frame, wt = lax.optimization_barrier((jnp.stack([own, far]), tab_own, raw, frame, wt))
    near = swap(both, 1)
    split = mine * 5 // 8 // 256 * 256
    parts = (split, mine - split)

    def sums(first, count, start, raw, todo, width):
        return call(
            functools.partial(sums_kernel, first, start),
            (shape((2, count, width), bf16), shape((4 * probes, count), f32), shape((4 * probes, count), bf16)),
            "sums",
            "v" * (3 + len(todo)),
            scratch=[VMEM((2, 256, width), f32)],
            flops=count * fl * (width // rows),
        )(frame, wt, raw, *todo)

    middle = [1 << j for j in range(1, bits - 1)]
    steps = len(middle)

    def exchange(x, j):
        turn = [middle[(j + core) % steps] for core in range(2)]
        return lax.ppermute(x, AXES, [(d, d ^ turn[d % 2]) for d in range(devices)])

    tab_far, raw_a = trig_call("trig_far", 0, split, far, raw)
    tab_a, acc_a, send_a = sums(0, parts[0], 0, raw_a, (near,), 2 * rows)
    tab_b, acc_b, send_b = sums(split, parts[1], split, raw, (far, near), 3 * rows)
    state = [[acc_a, send_a, None], [acc_b, send_b, None]]
    for j in range(steps):
        for chunk in range(2):
            acc, send, _ = state[chunk]
            got = exchange(send, j)
            if j + 1 < steps:
                acc = acc + got.astype(f32)
                send = acc.astype(bf16)
            state[chunk] = [acc, send, got]
    first = call(
        functools.partial(back_kernel, 0, (0, 0, 0), 256, False), shape((half, 4 * rows), f32), "back", "vvvvvv", flops=parts[0] * fl * 4
    )(state[0][0], state[0][2], frame, tab_own, tab_far, tab_a)
    keep, send = call(
        functools.partial(back_kernel, split, (split, 0), 256, True),
        (shape((half, 2 * rows), f32), shape((half, 2 * rows), bf16)),
        "back",
        "vvvvvv",
        flops=parts[1] * fl * 4,
    )(state[1][0], state[1][2], frame, tab_own, tab_b, first)
    there = swap(send, 1)
    keep = keep + there.astype(f32)
    there = swap(keep[:, rows:].astype(bf16), top)
    total = keep[:, :rows] + there.astype(f32)
    return total.reshape(forces.shape)


def solution(mesh):
    placed = (P(None, AXES), P(None, None, AXES), P())
    return jax.shard_map(
        shards,
        mesh=mesh,
        in_specs=placed,
        out_specs=P(None, None, AXES),
        check_vma=False,
    )
```

```python
import functools

import jax
import jax.numpy as jnp
from jax import lax
from jax.experimental import pallas as pl
from jax.experimental.pallas import tpu as pltpu
from jax.sharding import PartitionSpec as P

two_pi = 6.283185307179586
radius = 0.005
xi_split = 40.0
AXES = ("wide", "narrow")
VMEM = pltpu.VMEM
SMEM = pltpu.SMEM
f32, bf16 = jnp.float32, jnp.bfloat16

SIN = (4.4428676475109, -7.307433203747474, 3.5946900772135946, -0.7841130155066478)
STRIP = 32
PACE = 2
HEAD = 16


def horner(coeffs, q):
    total = coeffs[-1] * q + coeffs[-2]
    for c in reversed(coeffs[:-2]):
        total = total * q + c
    return total


def call(kernel, out_shape, name, specs, scratch=(), flops=0):
    many = isinstance(out_shape, (list, tuple))
    spaces = {"v": VMEM, "s": SMEM, "h": pltpu.HBM}
    return pl.pallas_call(
        kernel,
        out_shape=out_shape,
        in_specs=[pl.BlockSpec(memory_space=spaces[x]) for x in specs],
        out_specs=[pl.BlockSpec(memory_space=VMEM)] * len(out_shape) if many else pl.BlockSpec(memory_space=VMEM),
        scratch_shapes=scratch,
        name=name,
        compiler_params=pltpu.CompilerParams(vmem_limit_bytes=24 << 20),
        cost_estimate=pl.CostEstimate(flops=flops, bytes_accessed=flops // 256, transcendentals=0),
    )


def split3(x):
    hi = x.astype(bf16)
    rest = x - hi.astype(f32)
    mid = rest.astype(bf16)
    low = (rest - mid.astype(f32)).astype(bf16)
    return hi, mid, low


def pack_kernel(idx_ref, pos_hbm, force_hbm, waves_hbm, out_ref, own_ref, pos_ref, force_ref, sems):
    first = pl.multiple_of(idx_ref[0] * own_ref.shape[1], 128)
    copies = [
        pltpu.make_async_copy(pos_hbm, pos_ref, sems.at[0]),
        pltpu.make_async_copy(force_hbm, force_ref, sems.at[1]),
        pltpu.make_async_copy(waves_hbm.at[:, pl.ds(first, own_ref.shape[1])], own_ref, sems.at[2]),
    ]
    for copy in copies:
        copy.start()
    for copy in copies:
        copy.wait()
    hi, mid, low = split3(pos_ref[...])
    rows = out_ref.shape[1]
    parts = [hi.astype(f32), mid.astype(f32), low.astype(f32), jnp.zeros((HEAD - 9, rows), f32)]
    out_ref[:HEAD, :] = jnp.concatenate(parts, axis=0).astype(bf16)
    for a in range(force_ref.shape[0]):
        p = force_ref.shape[1]
        out_ref[HEAD + a * p : HEAD + (a + 1) * p, :] = force_ref[a].astype(bf16)


def frame_kernel(amp, own_ref, frame_ref, wt_ref):
    kwaves = own_ref.shape[1]
    m = own_ref[...].astype(f32)
    msq = jnp.sum(m * m, axis=0, keepdims=True)
    n = m * lax.rsqrt(msq)
    nx, ny, nz = n[0:1], n[1:2], n[2:3]
    sign = jnp.where(nz >= 0.0, 1.0, -1.0)
    a = -1.0 / (sign + nz)
    b = nx * ny * a
    ksq = (two_pi * two_pi) * msq
    qarg = ksq / (4.0 * xi_split * xi_split)
    factor = amp * (1.0 - radius * radius * ksq / 3.0) * (1.0 + qarg + 2.0 * qarg * qarg) * jnp.exp(-qarg) / ksq
    frame_ref[...] = jnp.concatenate(
        [1.0 + sign * nx * nx * a, sign * b, -sign * nx, b, sign + ny * ny * a, -ny, factor, jnp.zeros_like(b)], axis=0
    )
    head = jnp.concatenate([m, m, m, jnp.zeros((HEAD - 9, kwaves), f32)], axis=0)
    wt_ref[...] = jnp.transpose(head).astype(bf16)


def trig(u, tab_ref, rows, cols):
    r = u - jnp.round(u)
    s = r * horner(SIN, r * r)
    square = s * s
    tab_ref[0, rows, cols] = (1.0 - square).astype(bf16)
    rest = 2.0 - square
    tab_ref[1, rows, cols] = (s * (rest * lax.rsqrt(rest))).astype(bf16)


def runs_of(count):
    cuts = [*range(0, count, 256), count] if count % 256 else [*range(0, count - 256, 256), count - 256, count - 128, count]
    return [(a, b - a) for a, b in zip(cuts, cuts[1:])]


def tables(first, wt_ref, phase, tab_ref, u_ref, sum_up):
    width = phase.shape[1]
    lanes = min(width, 256)
    runs = runs_of(tab_ref.shape[1])

    def phases(n):
        base, count = runs[n]
        w = wt_ref[first + base : first + base + count, :]
        u_ref[n % 2, :count] = jnp.dot(w, phase, preferred_element_type=f32)

    phases(0)
    waiting = []
    for n, (base, count) in enumerate(runs):
        if n + 1 < len(runs):
            phases(n + 1)
        for row in range(0, count, STRIP):
            for low in range(0, width, lanes):
                cols = slice(low, low + lanes)
                trig(u_ref[n % 2, row : row + STRIP, cols], tab_ref, slice(base + row, base + row + STRIP), cols)
            if waiting and row // STRIP % PACE == 0:
                sum_up(*waiting.pop(0))
        waiting.extend((slice(base, base + count), part) for part in range(2))
    for late in waiting:
        sum_up(*late)


def product(force, table):
    return lax.dot_general(force, table, (((1,), (1,)), ((), ())), preferred_element_type=f32)


def trig_kernel(first, wt_ref, pack_ref, *refs):
    earlier, tab_ref, raw_ref, u_ref = refs if len(refs) == 4 else (None, *refs)
    half = pack_ref.shape[0] - HEAD
    phase, force = pack_ref[:HEAD], pack_ref[HEAD:]

    def sum_up(cols, part):
        rows = slice(part * half, (part + 1) * half)
        sums = product(force, tab_ref[part, cols, :])
        raw_ref[rows, cols] = sums if earlier is None else sums + earlier[rows, cols]

    tables(first, wt_ref, phase, tab_ref, u_ref, sum_up)


def unpacked(refs):
    blocks = []
    for ref in refs:
        blocks.extend([ref[...]] if len(ref.shape) == 2 else [ref[j] for j in range(ref.shape[0])])
    return blocks


def sums_kernel(first, start, frame_ref, wt_ref, raw_ref, *refs):
    todo = refs[:-4]
    tab_ref, acc_ref, send_ref, u_ref = refs[-4:]
    kwaves = tab_ref.shape[1]
    probes = acc_ref.shape[0] // 4
    half = 3 * probes
    blocks = unpacked(todo)
    phase = jnp.concatenate([b[:HEAD] for b in blocks], axis=1)
    forces = jnp.concatenate([b[HEAD:] for b in blocks], axis=1)

    def sum_up(cols, part):
        sums = product(forces, tab_ref[part, cols, :]) + raw_ref[part * half : (part + 1) * half, start + cols.start : start + cols.stop]
        fr = frame_ref[:, first + cols.start : first + cols.stop]
        for j in range(2):
            value = sum(fr[3 * j + x : 3 * j + x + 1] * sums[x * probes : (x + 1) * probes] for x in range(3))
            low = (2 * part + j) * probes
            acc_ref[low : low + probes, cols] = value
            send_ref[low : low + probes, cols] = value.astype(bf16)

    tables(first, wt_ref, phase, tab_ref, u_ref, sum_up)


def back_kernel(first, offsets, chunk, last, acc_ref, recv_ref, frame_ref, *refs):
    tables = refs[: len(offsets)]
    rest = refs[len(offsets) :]
    kwaves = acc_ref.shape[1]
    probes = acc_ref.shape[0] // 4
    halves = []
    for part in range(2):
        cols = slice(first, first + kwaves)
        t0, t1 = (
            frame_ref[6:7, cols] * (acc_ref[low : low + probes] + recv_ref[low : low + probes].astype(f32))
            for low in (2 * part * probes, (2 * part + 1) * probes)
        )
        halves.append(
            jnp.concatenate([frame_ref[x : x + 1, cols] * t0 + frame_ref[3 + x : 4 + x, cols] * t1 for x in range(3)], axis=0).astype(bf16)
        )
    begin = 0
    for offset, table in zip(offsets, tables):
        width = table.shape[2]
        total = sum(
            jnp.dot(halves[part], table[part, offset : offset + kwaves, :], preferred_element_type=f32) for part in range(2)
        )
        if not last:
            rest[0][:, begin : begin + width] = total
            begin += width
            continue
        earlier, keep, send = rest
        total += earlier[:, begin : begin + width]
        split = keep.shape[1]
        if begin < split:
            keep[:, begin : min(begin + width, split)] = total[:, : split - begin]
        if begin + width > split:
            low = max(begin, split)
            send[:, low - split : begin + width - split] = total[:, low - begin :].astype(bf16)
        begin += width


def shards(positions, forces, waves):
    wide, narrow = lax.axis_size("wide"), lax.axis_size("narrow")
    devices = wide * narrow
    bits = devices.bit_length() - 1
    assert devices == 1 << bits and bits >= 2
    rows = positions.shape[1]
    kwaves = waves.shape[1]
    half = forces.shape[0] * forces.shape[1]
    probes = forces.shape[1]
    top = devices >> 1
    amp = 20000.0 / float(rows * devices * kwaves) ** 0.5

    def swap(x, bit):
        return lax.ppermute(x, AXES, [(d, d ^ bit) for d in range(devices)])

    me = lax.axis_index(AXES)
    block = 2 * (me // top) + me % 2
    mine = kwaves // 4
    fl = 4 * half * rows
    shape = jax.ShapeDtypeStruct
    own, owned = call(
        pack_kernel,
        (shape((HEAD + half, rows), bf16), shape((3, mine), jnp.int32)),
        "pack",
        "shhh",
        scratch=[VMEM(positions.shape, f32), VMEM(forces.shape, f32), pltpu.SemaphoreType.DMA((3,))],
    )(block.reshape(1), *(pltpu.with_memory_space_constraint(x, pltpu.HBM) for x in (positions, forces, waves)))
    near = swap(own, 1)
    far = swap(own, top)
    frame, wt = call(
        functools.partial(frame_kernel, amp), (shape((8, mine), f32), shape((mine, HEAD), bf16)), "frame", "v", flops=mine * 1000
    )(owned)

    def trig_call(name, first, count, *operands):
        return call(
            functools.partial(trig_kernel, first),
            (shape((2, count, rows), bf16), shape((2 * half, count), f32)),
            name,
            "v" * (1 + len(operands)),
            scratch=[VMEM((2, 256, rows), f32)],
            flops=count * fl,
        )(wt, *operands)

    tab_own, raw = trig_call("trig_own", 0, mine, own)
    split = mine * 5 // 8 // 256 * 256
    parts = (split, mine - split)
    tab_near, raw_a = trig_call("trig_near", 0, split, near, raw)
    away, tab_near, raw_a = lax.optimization_barrier((far, tab_near, raw_a))
    across = swap(away, 1)

    def sums(first, count, start, raw, todo, width):
        return call(
            functools.partial(sums_kernel, first, start),
            (shape((2, count, width), bf16), shape((4 * probes, count), f32), shape((4 * probes, count), bf16)),
            "sums",
            "v" * (3 + len(todo)),
            scratch=[VMEM((2, 256, width), f32)],
            flops=count * fl * (width // rows),
        )(frame, wt, raw, *todo)

    middle = [1 << j for j in range(1, bits - 1)]
    steps = len(middle)

    def exchange(x, j):
        turn = [middle[(j + core) % steps] for core in range(2)]
        return lax.ppermute(x, AXES, [(d, d ^ turn[d % 2]) for d in range(devices)])

    tab_far, raw_a = trig_call("trig_far", 0, split, far, raw_a)
    tab_a, acc_a, send_a = sums(0, parts[0], 0, raw_a, (across,), rows)
    tab_b, acc_b, send_b = sums(split, parts[1], split, raw, (far, near, across), 3 * rows)
    state = [[acc_a, send_a, None], [acc_b, send_b, None]]
    for j in range(steps):
        for chunk in range(2):
            acc, send, _ = state[chunk]
            got = exchange(send, j)
            if j + 1 < steps:
                acc = acc + got.astype(f32)
                send = acc.astype(bf16)
            state[chunk] = [acc, send, got]
    first = call(
        functools.partial(back_kernel, 0, (0, 0, 0, 0), 256, False), shape((half, 4 * rows), f32), "back", "vvvvvvv", flops=parts[0] * fl * 4
    )(state[0][0], state[0][2], frame, tab_own, tab_far, tab_near, tab_a)
    keep, send = call(
        functools.partial(back_kernel, split, (split, 0), 256, True),
        (shape((half, 2 * rows), f32), shape((half, 2 * rows), bf16)),
        "back",
        "vvvvvv",
        flops=parts[1] * fl * 4,
    )(state[1][0], state[1][2], frame, tab_own, tab_b, first)
    there = swap(send, 1)
    keep = keep + there.astype(f32)
    there = swap(keep[:, rows:].astype(bf16), top)
    total = keep[:, :rows] + there.astype(f32)
    return total.reshape(forces.shape)


def solution(mesh):
    placed = (P(None, AXES), P(None, None, AXES), P())
    return jax.shard_map(
        shards,
        mesh=mesh,
        in_specs=placed,
        out_specs=P(None, None, AXES),
        check_vma=False,
    )
```

```python
import functools

import jax
import jax.numpy as jnp
from jax import lax
from jax.experimental import pallas as pl
from jax.experimental.pallas import tpu as pltpu
from jax.sharding import PartitionSpec as P

two_pi = 6.283185307179586
radius = 0.005
xi_split = 40.0
AXES = ("wide", "narrow")
VMEM = pltpu.VMEM
SMEM = pltpu.SMEM
f32, bf16 = jnp.float32, jnp.bfloat16

SIN = (4.4428676475109, -7.307433203747474, 3.5946900772135946, -0.7841130155066478)
STRIP = 32
PACE = 2
HEAD = 16


def horner(coeffs, q):
    total = coeffs[-1] * q + coeffs[-2]
    for c in reversed(coeffs[:-2]):
        total = total * q + c
    return total


def call(kernel, out_shape, name, specs, scratch=(), flops=0, aliases={}):
    many = isinstance(out_shape, (list, tuple))
    spaces = {"v": VMEM, "s": SMEM, "h": pltpu.HBM}
    return pl.pallas_call(
        kernel,
        out_shape=out_shape,
        in_specs=[pl.BlockSpec(memory_space=spaces[x]) for x in specs],
        out_specs=[pl.BlockSpec(memory_space=VMEM)] * len(out_shape) if many else pl.BlockSpec(memory_space=VMEM),
        scratch_shapes=scratch,
        name=name,
        input_output_aliases=aliases,
        compiler_params=pltpu.CompilerParams(vmem_limit_bytes=24 << 20),
        cost_estimate=pl.CostEstimate(flops=flops, bytes_accessed=flops // 256, transcendentals=0),
    )


def split3(x):
    hi = x.astype(bf16)
    rest = x - hi.astype(f32)
    mid = rest.astype(bf16)
    low = (rest - mid.astype(f32)).astype(bf16)
    return hi, mid, low


def pack_kernel(amp, idx_ref, pos_hbm, force_hbm, waves_hbm, out_ref, own_ref, frame_ref, wt_ref, pos_ref, force_ref, sems):
    first = pl.multiple_of(idx_ref[0] * own_ref.shape[1], 128)
    copies = [
        pltpu.make_async_copy(pos_hbm, pos_ref, sems.at[0]),
        pltpu.make_async_copy(force_hbm, force_ref, sems.at[1]),
        pltpu.make_async_copy(waves_hbm.at[:, pl.ds(first, own_ref.shape[1])], own_ref, sems.at[2]),
    ]
    for copy in copies:
        copy.start()
    for copy in copies:
        copy.wait()
    hi, mid, low = split3(pos_ref[...])
    rows = out_ref.shape[1]
    parts = [hi.astype(f32), mid.astype(f32), low.astype(f32), jnp.zeros((HEAD - 9, rows), f32)]
    out_ref[:HEAD, :] = jnp.concatenate(parts, axis=0).astype(bf16)
    for a in range(force_ref.shape[0]):
        p = force_ref.shape[1]
        out_ref[HEAD + a * p : HEAD + (a + 1) * p, :] = force_ref[a].astype(bf16)

    @pl.when(idx_ref[0] < 2)
    def _():
        frame_of(amp, own_ref, frame_ref, wt_ref)


def frame_kernel(amp, idx_ref, own_ref, frame_in, wt_in, frame_ref, wt_ref):
    @pl.when(idx_ref[0] >= 2)
    def _():
        frame_of(amp, own_ref, frame_ref, wt_ref)


def frame_of(amp, own_ref, frame_ref, wt_ref):
    kwaves = own_ref.shape[1]
    m = own_ref[...].astype(f32)
    msq = jnp.sum(m * m, axis=0, keepdims=True)
    n = m * lax.rsqrt(msq)
    nx, ny, nz = n[0:1], n[1:2], n[2:3]
    sign = jnp.where(nz >= 0.0, 1.0, -1.0)
    a = -1.0 / (sign + nz)
    b = nx * ny * a
    ksq = (two_pi * two_pi) * msq
    qarg = ksq / (4.0 * xi_split * xi_split)
    factor = amp * (1.0 - radius * radius * ksq / 3.0) * (1.0 + qarg + 2.0 * qarg * qarg) * jnp.exp(-qarg) / ksq
    frame_ref[...] = jnp.concatenate(
        [1.0 + sign * nx * nx * a, sign * b, -sign * nx, b, sign + ny * ny * a, -ny, factor, jnp.zeros_like(b)], axis=0
    )
    head = jnp.concatenate([m, m, m, jnp.zeros((HEAD - 9, kwaves), f32)], axis=0)
    wt_ref[...] = jnp.transpose(head).astype(bf16)


def trig(u, tab_ref, rows, cols):
    r = u - jnp.round(u)
    s = r * horner(SIN, r * r)
    square = s * s
    tab_ref[0, rows, cols] = (1.0 - square).astype(bf16)
    rest = 2.0 - square
    tab_ref[1, rows, cols] = (s * (rest * lax.rsqrt(rest))).astype(bf16)


def runs_of(count):
    cuts = [*range(0, count, 256), count] if count % 256 else [*range(0, count - 256, 256), count - 256, count - 128, count]
    return [(a, b - a) for a, b in zip(cuts, cuts[1:])]


def tables(first, wt_ref, phase, tab_ref, u_ref, sum_up):
    width = phase.shape[1]
    lanes = min(width, 256)
    runs = runs_of(tab_ref.shape[1])

    def phases(n):
        base, count = runs[n]
        w = wt_ref[first + base : first + base + count, :]
        u_ref[n % 2, :count] = jnp.dot(w, phase, preferred_element_type=f32)

    phases(0)
    waiting = []
    for n, (base, count) in enumerate(runs):
        if n + 1 < len(runs):
            phases(n + 1)
        for row in range(0, count, STRIP):
            for low in range(0, width, lanes):
                cols = slice(low, low + lanes)
                trig(u_ref[n % 2, row : row + STRIP, cols], tab_ref, slice(base + row, base + row + STRIP), cols)
            if waiting and row // STRIP % PACE == 0:
                sum_up(*waiting.pop(0))
        waiting.extend((slice(base, base + count), part) for part in range(2))
    for late in waiting:
        sum_up(*late)


def product(force, table):
    return lax.dot_general(force, table, (((1,), (1,)), ((), ())), preferred_element_type=f32)


def trig_kernel(first, wt_ref, pack_ref, *refs):
    earlier, tab_ref, raw_ref, u_ref = refs if len(refs) == 4 else (None, *refs)
    half = pack_ref.shape[0] - HEAD
    phase, force = pack_ref[:HEAD], pack_ref[HEAD:]

    def sum_up(cols, part):
        rows = slice(part * half, (part + 1) * half)
        sums = product(force, tab_ref[part, cols, :])
        raw_ref[rows, cols] = sums if earlier is None else sums + earlier[rows, cols]

    tables(first, wt_ref, phase, tab_ref, u_ref, sum_up)


def unpacked(refs):
    blocks = []
    for ref in refs:
        blocks.extend([ref[...]] if len(ref.shape) == 2 else [ref[j] for j in range(ref.shape[0])])
    return blocks


def sums_kernel(first, start, frame_ref, wt_ref, raw_ref, *refs):
    todo = refs[:-4]
    tab_ref, acc_ref, send_ref, u_ref = refs[-4:]
    kwaves = tab_ref.shape[1]
    probes = acc_ref.shape[0] // 4
    half = 3 * probes
    blocks = unpacked(todo)
    phase = jnp.concatenate([b[:HEAD] for b in blocks], axis=1)
    forces = jnp.concatenate([b[HEAD:] for b in blocks], axis=1)

    def sum_up(cols, part):
        sums = product(forces, tab_ref[part, cols, :]) + raw_ref[part * half : (part + 1) * half, start + cols.start : start + cols.stop]
        fr = frame_ref[:, first + cols.start : first + cols.stop]
        for j in range(2):
            value = sum(fr[3 * j + x : 3 * j + x + 1] * sums[x * probes : (x + 1) * probes] for x in range(3))
            low = (2 * part + j) * probes
            acc_ref[low : low + probes, cols] = value
            send_ref[low : low + probes, cols] = value.astype(bf16)

    tables(first, wt_ref, phase, tab_ref, u_ref, sum_up)


def back_kernel(first, pieces, earlier, acc_ref, recv_ref, frame_ref, *refs):
    kwaves = acc_ref.shape[1]
    probes = acc_ref.shape[0] // 4
    halves = []
    for part in range(2):
        cols = slice(first, first + kwaves)
        t0, t1 = (
            frame_ref[6:7, cols] * (acc_ref[low : low + probes] + recv_ref[low : low + probes].astype(f32))
            for low in (2 * part * probes, (2 * part + 1) * probes)
        )
        halves.append(
            jnp.concatenate([frame_ref[x : x + 1, cols] * t0 + frame_ref[3 + x : 4 + x, cols] * t1 for x in range(3)], axis=0).astype(bf16)
        )
    for table, row, low, before, out, begin, width in pieces:
        total = sum(
            jnp.dot(halves[part], refs[table][part, row : row + kwaves, low : low + width], preferred_element_type=f32)
            for part in range(2)
        )
        if earlier is not None:
            total += refs[earlier][:, before : before + width]
        refs[out][:, begin : begin + width] = total.astype(refs[out].dtype)


def shards(positions, forces, waves):
    wide, narrow = lax.axis_size("wide"), lax.axis_size("narrow")
    devices = wide * narrow
    bits = devices.bit_length() - 1
    assert devices == 1 << bits and bits >= 2
    rows = positions.shape[1]
    kwaves = waves.shape[1]
    half = forces.shape[0] * forces.shape[1]
    probes = forces.shape[1]
    top = devices >> 1
    amp = 20000.0 / float(rows * devices * kwaves) ** 0.5

    def swap(x, bit):
        return lax.ppermute(x, AXES, [(d, d ^ bit) for d in range(devices)])

    me = lax.axis_index(AXES)
    block = 2 * (me // top) + me % 2
    mine = kwaves // 4
    fl = 4 * half * rows
    shape = jax.ShapeDtypeStruct
    index = block.reshape(1)
    framed = (shape((8, mine), f32), shape((mine, HEAD), bf16))
    own, owned, frame, wt = call(
        functools.partial(pack_kernel, amp),
        (shape((HEAD + half, rows), bf16), shape((3, mine), jnp.int32), *framed),
        "pack",
        "shhh",
        scratch=[VMEM(positions.shape, f32), VMEM(forces.shape, f32), pltpu.SemaphoreType.DMA((3,))],
    )(index, *(pltpu.with_memory_space_constraint(x, pltpu.HBM) for x in (positions, forces, waves)))
    near = swap(own, 1)
    far = swap(own, top)
    frame, wt = call(
        functools.partial(frame_kernel, amp), framed, "frame", "svvv", flops=mine * 1000, aliases={2: 0, 3: 1}
    )(index, owned, frame, wt)

    def trig_call(name, first, count, *operands):
        return call(
            functools.partial(trig_kernel, first),
            (shape((2, count, rows), bf16), shape((2 * half, count), f32)),
            name,
            "v" * (1 + len(operands)),
            scratch=[VMEM((2, 256, rows), f32)],
            flops=count * fl,
        )(wt, *operands)

    tab_own, raw = trig_call("trig_own", 0, mine, own)
    split = mine * 5 // 8 // 256 * 256
    parts = (split, mine - split)
    tab_near, raw_a = trig_call("trig_near", 0, split, near, raw)
    away, tab_near, raw_a = lax.optimization_barrier((far, tab_near, raw_a))
    across = swap(away, 1)

    def sums(first, count, start, raw, todo, width):
        return call(
            functools.partial(sums_kernel, first, start),
            (shape((2, count, width), bf16), shape((4 * probes, count), f32), shape((4 * probes, count), bf16)),
            "sums",
            "v" * (3 + len(todo)),
            scratch=[VMEM((2, 256, width), f32)],
            flops=count * fl * (width // rows),
        )(frame, wt, raw, *todo)

    middle = [1 << j for j in range(1, bits - 1)]
    steps = len(middle)

    def exchange(x, j):
        turn = [middle[(j + core) % steps] for core in range(2)]
        return lax.ppermute(x, AXES, [(d, d ^ turn[d % 2]) for d in range(devices)])

    tab_far, raw_a = trig_call("trig_far", 0, split, far, raw_a)
    tab_a, acc_a, send_a = sums(0, parts[0], 0, raw_a, (across,), rows)
    tab_b, acc_b, send_b = sums(split, parts[1], split, raw, (far, near, across), 3 * rows)
    state = [[acc_a, send_a, None], [acc_b, send_b, None]]
    for j in range(steps):
        for chunk in range(2):
            acc, send, _ = state[chunk]
            got = exchange(send, j)
            if j + 1 < steps:
                acc = acc + got.astype(f32)
                send = acc.astype(bf16)
            state[chunk] = [acc, send, got]
    (acc_a, _, got_a), (acc_b, _, got_b) = state
    r = rows
    early = call(
        functools.partial(back_kernel, 0, [(j, 0, 0, 0, 4, j * r, r) for j in range(4)], None),
        shape((half, 4 * r), f32),
        "back",
        "vvvvvvv",
        flops=parts[0] * fl * 4,
    )(acc_a, got_a, frame, tab_own, tab_far, tab_near, tab_a)

    def late(keep, give):
        return call(
            functools.partial(back_kernel, split, [(*keep, 3, 0, r), (*give, 4, 0, r)], 2),
            (shape((half, r), f32), shape((half, r), bf16)),
            "back",
            "vvvvvv",
            flops=parts[1] * fl * 2,
        )(acc_b, got_b, frame, tab_own, tab_b, early)

    total_far, send_across = late((1, 0, 0, r), (1, 0, 2 * r, 3 * r))
    there = swap(send_across, 1)
    total, send_near = late((0, split, 0, 0), (1, 0, r, 2 * r))
    near_too = swap(send_near, 1)
    back = swap((total_far + there.astype(f32)).astype(bf16), top)
    total = total + near_too.astype(f32) + back.astype(f32)
    return total.reshape(forces.shape)


def solution(mesh):
    placed = (P(None, AXES), P(None, None, AXES), P())
    return jax.shard_map(
        shards,
        mesh=mesh,
        in_specs=placed,
        out_specs=P(None, None, AXES),
        check_vma=False,
    )
```

```python
import functools

import jax
import jax.numpy as jnp
from jax import lax
from jax.experimental import pallas as pl
from jax.experimental.pallas import tpu as pltpu
from jax.sharding import PartitionSpec as P

two_pi = 6.283185307179586
radius = 0.005
xi_split = 40.0
AXES = ("wide", "narrow")
VMEM = pltpu.VMEM
SMEM = pltpu.SMEM
f32, bf16 = jnp.float32, jnp.bfloat16

SIN = (4.4428676475109, -7.307433203747474, 3.5946900772135946, -0.7841130155066478)
STRIP = 32
PACE = 2
HEAD = 16


def horner(coeffs, q):
    total = coeffs[-1] * q + coeffs[-2]
    for c in reversed(coeffs[:-2]):
        total = total * q + c
    return total


def call(kernel, out_shape, name, specs, scratch=(), flops=0, aliases={}):
    many = isinstance(out_shape, (list, tuple))
    spaces = {"v": VMEM, "s": SMEM, "h": pltpu.HBM}
    return pl.pallas_call(
        kernel,
        out_shape=out_shape,
        in_specs=[pl.BlockSpec(memory_space=spaces[x]) for x in specs],
        out_specs=[pl.BlockSpec(memory_space=VMEM)] * len(out_shape) if many else pl.BlockSpec(memory_space=VMEM),
        scratch_shapes=scratch,
        name=name,
        input_output_aliases=aliases,
        compiler_params=pltpu.CompilerParams(vmem_limit_bytes=24 << 20),
        cost_estimate=pl.CostEstimate(flops=flops, bytes_accessed=flops // 256, transcendentals=0),
    )


def split3(x):
    hi = x.astype(bf16)
    rest = x - hi.astype(f32)
    mid = rest.astype(bf16)
    low = (rest - mid.astype(f32)).astype(bf16)
    return hi, mid, low


def pack_kernel(amp, idx_ref, pos_hbm, force_hbm, waves_hbm, out_ref, own_ref, frame_ref, wt_ref, pos_ref, force_ref, sems):
    first = pl.multiple_of(idx_ref[0] * own_ref.shape[1], 128)
    copies = [
        pltpu.make_async_copy(pos_hbm, pos_ref, sems.at[0]),
        pltpu.make_async_copy(force_hbm, force_ref, sems.at[1]),
        pltpu.make_async_copy(waves_hbm.at[:, pl.ds(first, own_ref.shape[1])], own_ref, sems.at[2]),
    ]
    for copy in copies:
        copy.start()
    for copy in copies:
        copy.wait()
    hi, mid, low = split3(pos_ref[...])
    rows = out_ref.shape[1]
    parts = [hi.astype(f32), mid.astype(f32), low.astype(f32), jnp.zeros((HEAD - 9, rows), f32)]
    out_ref[:HEAD, :] = jnp.concatenate(parts, axis=0).astype(bf16)
    for a in range(force_ref.shape[0]):
        p = force_ref.shape[1]
        out_ref[HEAD + a * p : HEAD + (a + 1) * p, :] = force_ref[a].astype(bf16)

    @pl.when(idx_ref[0] < 2)
    def _():
        frame_of(amp, own_ref, frame_ref, wt_ref)


def frame_kernel(amp, idx_ref, own_ref, frame_in, wt_in, frame_ref, wt_ref):
    @pl.when(idx_ref[0] >= 2)
    def _():
        frame_of(amp, own_ref, frame_ref, wt_ref)


def frame_of(amp, own_ref, frame_ref, wt_ref):
    kwaves = own_ref.shape[1]
    m = own_ref[...].astype(f32)
    msq = jnp.sum(m * m, axis=0, keepdims=True)
    n = m * lax.rsqrt(msq)
    nx, ny, nz = n[0:1], n[1:2], n[2:3]
    sign = jnp.where(nz >= 0.0, 1.0, -1.0)
    a = -1.0 / (sign + nz)
    b = nx * ny * a
    ksq = (two_pi * two_pi) * msq
    qarg = ksq / (4.0 * xi_split * xi_split)
    factor = amp * (1.0 - radius * radius * ksq / 3.0) * (1.0 + qarg + 2.0 * qarg * qarg) * jnp.exp(-qarg) / ksq
    frame_ref[...] = jnp.concatenate(
        [1.0 + sign * nx * nx * a, sign * b, -sign * nx, b, sign + ny * ny * a, -ny, factor, jnp.zeros_like(b)], axis=0
    )
    head = jnp.concatenate([m, m, m, jnp.zeros((HEAD - 9, kwaves), f32)], axis=0)
    wt_ref[...] = jnp.transpose(head).astype(bf16)


def trig(u, tab_ref, rows, cols):
    r = u - jnp.round(u)
    s = r * horner(SIN, r * r)
    square = s * s
    tab_ref[0, rows, cols] = (1.0 - square).astype(bf16)
    rest = 2.0 - square
    tab_ref[1, rows, cols] = (s * (rest * lax.rsqrt(rest))).astype(bf16)


def runs_of(count):
    cuts = [*range(0, count, 256), count] if count % 256 else [*range(0, count - 256, 256), count - 256, count - 128, count]
    return [(a, b - a) for a, b in zip(cuts, cuts[1:])]


def tables(first, wt_ref, phase, tab_ref, u_ref, sum_up):
    width = phase.shape[1]
    lanes = min(width, 256)
    runs = runs_of(tab_ref.shape[1])

    def phases(n):
        base, count = runs[n]
        w = wt_ref[first + base : first + base + count, :]
        u_ref[n % 2, :count] = jnp.dot(w, phase, preferred_element_type=f32)

    phases(0)
    waiting = []
    for n, (base, count) in enumerate(runs):
        if n + 1 < len(runs):
            phases(n + 1)
        for row in range(0, count, STRIP):
            for low in range(0, width, lanes):
                cols = slice(low, low + lanes)
                trig(u_ref[n % 2, row : row + STRIP, cols], tab_ref, slice(base + row, base + row + STRIP), cols)
            if waiting and row // STRIP % PACE == 0:
                sum_up(*waiting.pop(0))
        waiting.extend((slice(base, base + count), part) for part in range(2))
    for late in waiting:
        sum_up(*late)


def product(force, table):
    return lax.dot_general(force, table, (((1,), (1,)), ((), ())), preferred_element_type=f32)


def trig_kernel(first, wt_ref, pack_ref, *refs):
    earlier, tab_ref, raw_ref, u_ref = refs if len(refs) == 4 else (None, *refs)
    half = pack_ref.shape[0] - HEAD
    phase, force = pack_ref[:HEAD], pack_ref[HEAD:]

    def sum_up(cols, part):
        rows = slice(part * half, (part + 1) * half)
        sums = product(force, tab_ref[part, cols, :])
        raw_ref[rows, cols] = sums if earlier is None else sums + earlier[rows, cols]

    tables(first, wt_ref, phase, tab_ref, u_ref, sum_up)


def unpacked(refs):
    blocks = []
    for ref in refs:
        blocks.extend([ref[...]] if len(ref.shape) == 2 else [ref[j] for j in range(ref.shape[0])])
    return blocks


def sums_kernel(first, start, frame_ref, wt_ref, raw_ref, *refs):
    todo = refs[:-4]
    tab_ref, acc_ref, send_ref, u_ref = refs[-4:]
    kwaves = tab_ref.shape[1]
    probes = acc_ref.shape[0] // 4
    half = 3 * probes
    blocks = unpacked(todo)
    phase = jnp.concatenate([b[:HEAD] for b in blocks], axis=1)
    forces = jnp.concatenate([b[HEAD:] for b in blocks], axis=1)

    def sum_up(cols, part):
        sums = product(forces, tab_ref[part, cols, :]) + raw_ref[part * half : (part + 1) * half, start + cols.start : start + cols.stop]
        fr = frame_ref[:, first + cols.start : first + cols.stop]
        for j in range(2):
            value = sum(fr[3 * j + x : 3 * j + x + 1] * sums[x * probes : (x + 1) * probes] for x in range(3))
            low = (2 * part + j) * probes
            acc_ref[low : low + probes, cols] = value
            send_ref[low : low + probes, cols] = value.astype(bf16)

    tables(first, wt_ref, phase, tab_ref, u_ref, sum_up)


def back_kernel(first, pieces, earlier, acc_ref, recv_ref, frame_ref, *refs):
    kwaves = acc_ref.shape[1]
    probes = acc_ref.shape[0] // 4
    halves = []
    for part in range(2):
        cols = slice(first, first + kwaves)
        t0, t1 = (
            frame_ref[6:7, cols] * (acc_ref[low : low + probes] + recv_ref[low : low + probes].astype(f32))
            for low in (2 * part * probes, (2 * part + 1) * probes)
        )
        halves.append(
            jnp.concatenate([frame_ref[x : x + 1, cols] * t0 + frame_ref[3 + x : 4 + x, cols] * t1 for x in range(3)], axis=0).astype(bf16)
        )
    for table, row, low, before, out, begin, width in pieces:
        total = sum(
            jnp.dot(halves[part], refs[table][part, row : row + kwaves, low : low + width], preferred_element_type=f32)
            for part in range(2)
        )
        if earlier is not None:
            total += refs[earlier][:, before : before + width]
        refs[out][:, begin : begin + width] = total.astype(refs[out].dtype)


def shards(positions, forces, waves):
    wide, narrow = lax.axis_size("wide"), lax.axis_size("narrow")
    devices = wide * narrow
    bits = devices.bit_length() - 1
    assert devices == 1 << bits and bits >= 2
    rows = positions.shape[1]
    kwaves = waves.shape[1]
    half = forces.shape[0] * forces.shape[1]
    probes = forces.shape[1]
    top = devices >> 1
    amp = 20000.0 / float(rows * devices * kwaves) ** 0.5

    def swap(x, bit):
        return lax.ppermute(x, AXES, [(d, d ^ bit) for d in range(devices)])

    me = lax.axis_index(AXES)
    block = 2 * (me // top) + me % 2
    mine = kwaves // 4
    fl = 4 * half * rows
    shape = jax.ShapeDtypeStruct
    index = block.reshape(1)
    framed = (shape((8, mine), f32), shape((mine, HEAD), bf16))
    own, owned, frame, wt = call(
        functools.partial(pack_kernel, amp),
        (shape((HEAD + half, rows), bf16), shape((3, mine), jnp.int32), *framed),
        "pack",
        "shhh",
        scratch=[VMEM(positions.shape, f32), VMEM(forces.shape, f32), pltpu.SemaphoreType.DMA((3,))],
    )(index, *(pltpu.with_memory_space_constraint(x, pltpu.HBM) for x in (positions, forces, waves)))
    near = swap(own, 1)
    far = swap(own, top)
    frame, wt = call(
        functools.partial(frame_kernel, amp), framed, "frame", "svvv", flops=mine * 1000, aliases={2: 0, 3: 1}
    )(index, owned, frame, wt)

    def trig_call(name, first, count, *operands):
        return call(
            functools.partial(trig_kernel, first),
            (shape((2, count, rows), bf16), shape((2 * half, count), f32)),
            name,
            "v" * (1 + len(operands)),
            scratch=[VMEM((2, 256, rows), f32)],
            flops=count * fl,
        )(wt, *operands)

    tab_own, raw = trig_call("trig_own", 0, mine, own)
    split = mine * 5 // 8 // 256 * 256
    parts = (split, mine - split)
    tab_near, raw_a = trig_call("trig_near", 0, split, near, raw)
    away, tab_near, raw_a = lax.optimization_barrier((far, tab_near, raw_a))
    across = swap(away, 1)

    def sums(first, count, start, raw, todo, width):
        return call(
            functools.partial(sums_kernel, first, start),
            (shape((2, count, width), bf16), shape((4 * probes, count), f32), shape((4 * probes, count), bf16)),
            "sums",
            "v" * (3 + len(todo)),
            scratch=[VMEM((2, 256, width), f32)],
            flops=count * fl * (width // rows),
        )(frame, wt, raw, *todo)

    middle = [1 << j for j in range(1, bits - 1)]
    steps = len(middle)

    def exchange(x, j):
        turn = [middle[(j + core) % steps] for core in range(2)]
        return lax.ppermute(x, AXES, [(d, d ^ turn[d % 2]) for d in range(devices)])

    tab_far, raw_a = trig_call("trig_far", 0, split, far, raw_a)
    tab_a, acc_a, send_a = sums(0, parts[0], 0, raw_a, (across,), rows)
    tab_b, acc_b, send_b = sums(split, parts[1], split, raw, (far, near, across), 3 * rows)
    state = [[acc_a, send_a, None], [acc_b, send_b, None]]
    for j in range(steps):
        for chunk in range(2):
            acc, send, _ = state[chunk]
            got = exchange(send, j)
            if j + 1 < steps:
                acc = acc + got.astype(f32)
                send = acc.astype(bf16)
            state[chunk] = [acc, send, got]
    (acc_a, _, got_a), (acc_b, _, got_b) = state
    r = rows
    early = call(
        functools.partial(back_kernel, 0, [(j, 0, 0, 0, 4, j * r, r) for j in range(4)], None),
        shape((half, 4 * r), f32),
        "back",
        "vvvvvvv",
        flops=parts[0] * fl * 4,
    )(acc_a, got_a, frame, tab_own, tab_far, tab_near, tab_a)

    def late(pieces, *outs):
        return call(
            functools.partial(back_kernel, split, [(*piece, 3 + j, 0, r) for j, piece in enumerate(pieces)], 2),
            [shape((half, r), kind) for kind in outs],
            "back",
            "vvvvvv",
            flops=parts[1] * fl * len(outs),
        )(acc_b, got_b, frame, tab_own, tab_b, early)

    (send_across,) = late([(1, 0, 2 * r, 3 * r)], bf16)
    there = swap(send_across, 1)
    total_far, total, send_near = late([(1, 0, 0, r), (0, split, 0, 0), (1, 0, r, 2 * r)], f32, f32, bf16)
    near_too = swap(send_near, 1)
    back = swap((total_far + there.astype(f32)).astype(bf16), top)
    total = total + near_too.astype(f32) + back.astype(f32)
    return total.reshape(forces.shape)


def solution(mesh):
    placed = (P(None, AXES), P(None, None, AXES), P())
    return jax.shard_map(
        shards,
        mesh=mesh,
        in_specs=placed,
        out_specs=P(None, None, AXES),
        check_vma=False,
    )
```
